32 devices in a mesh: dp: 8 (over z, y), mp: 4 (over x, core).
Axes of the slice: x: 2, y: 2, z: 4, core: 2. Of those that a mesh axis runs over, the one named last changes fastest.
Arguments:
- block_input: float32 [4096, 768], P(('dp', 'mp')), may hold values from -54 to 54
- out_cotangent: float32 [4096, 768], P(('dp', 'mp')), may hold values from -6 to 6
- gain_attend: float32 [768], P('dp'), may hold values from 0.5 to 1.5
- weight_triple: float32 [3, 768, 768], P(None, 'dp', 'mp'), may hold values from -4 to 4
- weight_merge: float32 [768, 768], P('mp', 'dp'), may hold values from -0.875 to 0.875
- gain_feed: float32 [768], P('dp'), may hold values from 0.5 to 1.5
- weight_expand: float32 [2, 768, 1152], P(None, 'dp', 'mp'), may hold values from -0.21875 to 0.21875
- weight_reduce: float32 [1152, 768], P('mp', 'dp'), may hold values from -0.1875 to 0.1875
- mean_attend: float32 [768], P('dp'), may hold values from -40 to 40
- mean_triple: float32 [3, 768, 768], P(None, 'dp', 'mp'), may hold values from -40 to 40
- mean_merge: float32 [768, 768], P('mp', 'dp'), may hold values from -40 to 40
- mean_feed: float32 [768], P('dp'), may hold values from -40 to 40
- mean_expand: float32 [2, 768, 1152], P(None, 'dp', 'mp'), may hold values from -40 to 40
- mean_reduce: float32 [1152, 768], P('mp', 'dp'), may hold values from -40 to 40
- square_attend: float32 [768], P('dp'), may hold values from 1.3653333 to 13.653334
- square_triple: float32 [3, 768, 768], P(None, 'dp', 'mp'), may hold values from 1.3653333 to 13.653334
- square_merge: float32 [768, 768], P('mp', 'dp'), may hold values from 1.3653333 to 13.653334
- square_feed: float32 [768], P('dp'), may hold values from 1.3653333 to 13.653334
- square_expand: float32 [2, 768, 1152], P(None, 'dp', 'mp'), may hold values from 1.3653333 to 13.653334
- square_reduce: float32 [1152, 768], P('mp', 'dp'), may hold values from 1.3653333 to 13.653334
Outputs:
- block_output: float32 [4096, 768], P(('dp', 'mp'))
- input_grad: float32 [4096, 768], P(('dp', 'mp'))
- grad_attend: float32 [768], P('dp')
- grad_triple: float32 [3, 768, 768], P(None, 'dp', 'mp')
- grad_merge: float32 [768, 768], P('mp', 'dp')
- grad_feed: float32 [768], P('dp')
- grad_expand: float32 [2, 768, 1152], P(None, 'dp', 'mp')
- grad_reduce: float32 [1152, 768], P('mp', 'dp')
- fresh_attend: float32 [768], P('dp')
- fresh_triple: float32 [3, 768, 768], P(None, 'dp', 'mp')
- fresh_merge: float32 [768, 768], P('mp', 'dp')
- fresh_feed: float32 [768], P('dp')
- fresh_expand: float32 [2, 768, 1152], P(None, 'dp', 'mp')
- fresh_reduce: float32 [1152, 768], P('mp', 'dp')
- first_attend: float32 [768], P('dp')
- first_triple: float32 [3, 768, 768], P(None, 'dp', 'mp')
- first_merge: float32 [768, 768], P('mp', 'dp')
- first_feed: float32 [768], P('dp')
- first_expand: float32 [2, 768, 1152], P(None, 'dp', 'mp')
- first_reduce: float32 [1152, 768], P('mp', 'dp')
- second_attend: float32 [768], P('dp')
- second_triple: float32 [3, 768, 768], P(None, 'dp', 'mp')
- second_merge: float32 [768, 768], P('mp', 'dp')
- second_feed: float32 [768], P('dp')
- second_expand: float32 [2, 768, 1152], P(None, 'dp', 'mp')
- second_reduce: float32 [1152, 768], P('mp', 'dp')
The draws below stay inside these ranges and needn't reach their ends.
All inputs are finite; a program needn't handle non-finite values.
Results may differ from the reference program's by a relative error of at most 0.017.
Values may be sent and summed in bfloat16 or wider, within the bound.
No kernel may reach another device: no remote copies, remote signals or barrier semaphores. Data moves between devices by JAX's collectives and lax.ppermute only.
A program may use at most 64 MiB of HBM per device.

```python
import math
from functools import partial
import jax
import jax.numpy as jnp
from jax import lax

D = 768
HEADS = 12
HD = 64
FF = 1152
WINDOW = 128
LEN = 512
TOKENS = 4096


def draw_block_input(key, part):
    base_key, row_key, column_key = jax.random.split(key, 3)
    row_scale = jnp.exp(jax.random.uniform(row_key, (TOKENS, 1), jnp.float32, math.log(0.3), math.log(3.0)))
    column_scale = jnp.exp(jax.random.uniform(column_key, (1, D), jnp.float32, math.log(0.3), math.log(3.0)))
    base_draw = jnp.clip(jax.random.normal(base_key, (TOKENS, D), jnp.float32), -6.0, 6.0)
    return base_draw * row_scale * column_scale


def draw_weight_triple(key, part):
    base_draw = jnp.clip(jax.random.normal(key, (3, D, D), jnp.float32), -6.0, 6.0) / math.sqrt(D)
    return jnp.clip(base_draw, -4.0, 4.0)


def level_of(own_key, dims, cuts, low, largest):
    loudness, own = 1.0, jax.random.fold_in(own_key, 6)
    for position, shards_of in cuts:
        steps = jnp.exp(jax.random.uniform(jax.random.fold_in(own, position), (shards_of,), jnp.float32, low / len(cuts), largest / len(cuts)))
        loudness = loudness * jnp.repeat(steps, dims[position] // shards_of).reshape([-1 if axis == position else 1 for axis in range(len(dims))])
    return loudness


def centred(key, extent, spread, reach, shards=(), held_as=jnp.bfloat16):
    level = level_of(key, extent, shards, -0.22, 0.18) if shards else 1.0
    result = jax.random.normal(key, extent, jnp.float32) * spread * level
    return jnp.minimum(jnp.maximum(result, -reach), reach).astype(held_as)


def setup_inputs(seed: int = 0) -> dict:
    key_of = jax.random.split(jax.random.key(seed), 21)
    return {
        "block_input": draw_block_input(jax.random.fold_in(key_of[20], 71), 0),
        "out_cotangent": centred(key_of[1], (TOKENS, D), 1.0, 6.0, ((0, 32),), jnp.float32),
        "gain_attend": jnp.clip(1.0 + 0.1 * jax.random.normal(key_of[2], (D,), jnp.float32), 0.5, 1.5),
        "weight_triple": draw_weight_triple(jax.random.fold_in(key_of[20], 71), 0),
        "weight_merge": centred(key_of[4], (D, D), (D // 16) ** -0.5, 0.875, ((0, 4), (1, 8)), jnp.float32),
        "gain_feed": jnp.clip(1.0 + 0.1 * jax.random.normal(key_of[5], (D,), jnp.float32), 0.5, 1.5),
        "weight_expand": centred(key_of[6], (2, D, FF), D ** -0.5, 0.21875, ((1, 8), (2, 4)), jnp.float32),
        "weight_reduce": centred(key_of[7], (FF, D), FF ** -0.5, 0.1875, ((0, 4), (1, 8)), jnp.float32),
        "mean_attend": centred(key_of[8], (D,), (TOKENS ** 0.5 / 9), 40.0, ((0, 8),), jnp.float32),
        "mean_triple": centred(key_of[9], (3, D, D), (TOKENS ** 0.5 / 9), 40.0, ((1, 8), (2, 4)), jnp.float32),
        "mean_merge": centred(key_of[10], (D, D), (TOKENS ** 0.5 / 9), 40.0, ((0, 4), (1, 8)), jnp.float32),
        "mean_feed": centred(key_of[11], (D,), (TOKENS ** 0.5 / 9), 40.0, ((0, 8),), jnp.float32),
        "mean_expand": centred(key_of[12], (2, D, FF), (TOKENS ** 0.5 / 9), 40.0, ((1, 8), (2, 4)), jnp.float32),
        "mean_reduce": centred(key_of[13], (FF, D), (TOKENS ** 0.5 / 9), 40.0, ((0, 4), (1, 8)), jnp.float32),
        "square_attend": jnp.clip(jnp.exp(math.log(13.653334) - 2.3025851 * jax.random.uniform(key_of[14], (D,), jnp.float32) ** level_of(key_of[14], (D,), ((0, 8),), -0.2, 0.2)), 1.3653333, 13.653334),
        "square_triple": jnp.clip(jnp.exp(math.log(13.653334) - 2.3025851 * jax.random.uniform(key_of[15], (3, D, D), jnp.float32) ** level_of(key_of[15], (3, D, D), ((1, 8), (2, 4)), -0.2, 0.2)), 1.3653333, 13.653334),
        "square_merge": jnp.clip(jnp.exp(math.log(13.653334) - 2.3025851 * jax.random.uniform(key_of[16], (D, D), jnp.float32) ** level_of(key_of[16], (D, D), ((0, 4), (1, 8)), -0.2, 0.2)), 1.3653333, 13.653334),
        "square_feed": jnp.clip(jnp.exp(math.log(13.653334) - 2.3025851 * jax.random.uniform(key_of[17], (D,), jnp.float32) ** level_of(key_of[17], (D,), ((0, 8),), -0.2, 0.2)), 1.3653333, 13.653334),
        "square_expand": jnp.clip(jnp.exp(math.log(13.653334) - 2.3025851 * jax.random.uniform(key_of[18], (2, D, FF), jnp.float32) ** level_of(key_of[18], (2, D, FF), ((1, 8), (2, 4)), -0.2, 0.2)), 1.3653333, 13.653334),
        "square_reduce": jnp.clip(jnp.exp(math.log(13.653334) - 2.3025851 * jax.random.uniform(key_of[19], (FF, D), jnp.float32) ** level_of(key_of[19], (FF, D), ((0, 4), (1, 8)), -0.2, 0.2)), 1.3653333, 13.653334),
    }


NORM_EPS = 1e-05
ROPE_BASE = 10000.0
BETA_FIRST = 0.9
BETA_SECOND = 0.999
ADAM_EPS = 1e-08
DECAY = 0.01
RATE_MATRIX = 0.02
RATE_GAIN = 0.2
STEP_COUNT = 3.0
MASKED = -1e+30
TILE_ROWS = 128

def normalize(rows_in):
    center = rows_in - lax.optimization_barrier(jnp.mean(rows_in, axis=-1, keepdims=True))
    scale = lax.rsqrt(lax.optimization_barrier(jnp.mean(center * center, axis=-1, keepdims=True)) + NORM_EPS)
    return (center * scale, scale)

def norm_back(grad_in, normed, scale, gain):
    scaled = grad_in * gain
    return scale * (scaled - lax.optimization_barrier(jnp.mean(scaled, axis=-1, keepdims=True)) - normed * lax.optimization_barrier(jnp.mean(scaled * normed, axis=-1, keepdims=True)))

def rope_tables(length, size):
    half = size // 2
    freqs = jnp.power(jnp.float32(ROPE_BASE), -2.0 * jnp.arange(half, dtype=jnp.float32) / size)
    angles = jnp.arange(length, dtype=jnp.float32)[:, None] * freqs[None, :]
    return (jnp.cos(angles)[:, None, :], jnp.sin(angles)[:, None, :])

def rotate(field, cosine, sine):
    half = field.shape[-1] // 2
    first, second = (field[..., :half], field[..., half:])
    return jnp.concatenate([first * cosine - second * sine, second * cosine + first * sine], axis=-1)

def rotate_back(grad, cosine, sine):
    half = grad.shape[-1] // 2
    first, second = (grad[..., :half], grad[..., half:])
    return jnp.concatenate([first * cosine + second * sine, second * cosine - first * sine], axis=-1)

def gelu_parts(value):
    normal_share = 0.5 * (1.0 + lax.erf(value * (1.0 / math.sqrt(2.0))))
    density = jnp.exp(-0.5 * value * value) * (1.0 / math.sqrt(2.0 * math.pi))
    return (value * normal_share, normal_share + value * density)

def contract_rows(left, right):
    return lax.dot_general(left.astype(jnp.float32), right.astype(jnp.float32), (((0,), (0,)), ((), ())), preferred_element_type=jnp.float32)

def against(left, weight):
    return lax.dot_general(left.astype(jnp.float32), weight.astype(jnp.float32), (((1,), (1,)), ((), ())), preferred_element_type=jnp.float32)

def window_mask(start, block, width, length):
    half = (width - block) // 2
    query_pos = start + jnp.arange(block)
    key_pos = start - half + jnp.arange(width)
    near = jnp.abs(query_pos[:, None] - key_pos[None, :]) <= half
    inside = (key_pos >= 0) & (key_pos < length)
    return near & inside[None, :]

def tile_layout(length):
    half = WINDOW // 2
    width = TILE_ROWS + 2 * half
    outer = min(length, 512)
    return (half, width, outer, outer // TILE_ROWS)

def stack_tiles(padded, starts, width):
    return jnp.stack([padded[begin:begin + width] for begin in starts])

def tile_scores(query_tiles, key_tiles, starts, width, length, scale):
    scores = jnp.einsum('bqhd,bkhd->hbqk', query_tiles.astype(jnp.float32), key_tiles.astype(jnp.float32)) * scale
    masks = jnp.stack([window_mask(begin, TILE_ROWS, width, length) for begin in starts])
    return jnp.where(masks[None], scores, MASKED)

def attend(query, keys, values):
    length, heads, size = query.shape
    half, width, outer, count = tile_layout(length)
    scale = 1.0 / math.sqrt(size)
    pad_keys = jnp.pad(keys, ((half, half), (0, 0), (0, 0)))
    pad_values = jnp.pad(values, ((half, half), (0, 0), (0, 0)))
    outputs = []
    totals = []
    for start in range(0, length, outer):
        starts = [start + k * TILE_ROWS for k in range(count)]
        query_tiles = query[start:start + outer].reshape(count, TILE_ROWS, heads, size)
        key_tiles = stack_tiles(pad_keys, starts, width)
        value_tiles = stack_tiles(pad_values, starts, width)
        scores = tile_scores(query_tiles, key_tiles, starts, width, length, scale)
        top = lax.optimization_barrier(jnp.max(scores, axis=-1, keepdims=True))
        total = top + jnp.log(lax.optimization_barrier(jnp.sum(jnp.exp(scores - top), axis=-1, keepdims=True)))
        probs = jnp.exp(scores - total).astype(jnp.bfloat16)
        out_tiles = jnp.einsum('hbqk,bkhd->bqhd', probs.astype(jnp.float32), value_tiles.astype(jnp.float32))
        outputs.append(out_tiles.reshape(outer, heads, size).astype(jnp.bfloat16))
        totals.append(total[..., 0].reshape(heads, outer))
    return (jnp.concatenate(outputs, 0), jnp.concatenate(totals, 1))

def attend_back(query, keys, values, attended, totals, d_attended):
    length, heads, size = query.shape
    half, width, outer, count = tile_layout(length)
    scale = 1.0 / math.sqrt(size)
    pad_keys = jnp.pad(keys, ((half, half), (0, 0), (0, 0)))
    pad_values = jnp.pad(values, ((half, half), (0, 0), (0, 0)))
    grad_keys = jnp.zeros((length + 2 * half, heads, size), jnp.float32)
    grad_values = jnp.zeros((length + 2 * half, heads, size), jnp.float32)
    grad_query = []
    for start in range(0, length, outer):
        starts = [start + k * TILE_ROWS for k in range(count)]
        query_tiles = query[start:start + outer].reshape(count, TILE_ROWS, heads, size)
        key_tiles = stack_tiles(pad_keys, starts, width)
        value_tiles = stack_tiles(pad_values, starts, width).astype(jnp.float32)
        back_tiles = d_attended[start:start + outer].reshape(count, TILE_ROWS, heads, size).astype(jnp.float32)
        kept_tiles = attended[start:start + outer].reshape(count, TILE_ROWS, heads, size).astype(jnp.float32)
        scores = tile_scores(query_tiles, key_tiles, starts, width, length, scale)
        lse_tiles = totals[:, start:start + outer].reshape(heads, count, TILE_ROWS)[..., None]
        probs = jnp.exp(scores - lse_tiles)
        probs_b = probs.astype(jnp.bfloat16).astype(jnp.float32)
        d_probs = jnp.einsum('bqhd,bkhd->hbqk', back_tiles, value_tiles)
        delta = jnp.transpose(lax.optimization_barrier(jnp.sum(back_tiles * kept_tiles, axis=-1)), (2, 0, 1))
        d_scores = (probs * (d_probs - delta[..., None]) * scale).astype(jnp.bfloat16).astype(jnp.float32)
        grad_query.append(jnp.einsum('hbqk,bkhd->bqhd', d_scores, key_tiles.astype(jnp.float32)).reshape(outer, heads, size))
        key_parts = jnp.einsum('hbqk,bqhd->bkhd', d_scores, query_tiles.astype(jnp.float32))
        value_parts = jnp.einsum('hbqk,bqhd->bkhd', probs_b, back_tiles)
        for k in range(count):
            begin = starts[k]
            grad_keys = grad_keys.at[begin:begin + width].add(key_parts[k])
            grad_values = grad_values.at[begin:begin + width].add(value_parts[k])
    return (jnp.concatenate(grad_query, 0), grad_keys[half:half + length], grad_values[half:half + length])

def round_gain(gain):
    return lax.optimization_barrier(gain.astype(jnp.bfloat16)).astype(jnp.float32)

def sequence_pass(params, grads, pieces):
    gain_one, triple_b, merge_b, gain_two, expand_b, reduce_b = params
    rows_in, cotangent = pieces
    length = rows_in.shape[0]
    cosine, sine = rope_tables(length, HD)
    normed_one, rstd_one = normalize(rows_in)
    hidden_one = (normed_one * gain_one).astype(jnp.bfloat16)
    pre = jnp.einsum('sd,cdf->csf', hidden_one.astype(jnp.float32), triple_b.astype(jnp.float32))
    query = rotate(pre[0].reshape(length, HEADS, HD), cosine, sine).astype(jnp.bfloat16)
    keys = rotate(pre[1].reshape(length, HEADS, HD), cosine, sine).astype(jnp.bfloat16)
    values = pre[2].reshape(length, HEADS, HD).astype(jnp.bfloat16)
    attended, totals = attend(query, keys, values)
    attended_flat = attended.reshape(length, D)
    residual = rows_in + jnp.dot(attended_flat, merge_b, preferred_element_type=jnp.float32)
    normed_two, rstd_two = normalize(residual)
    hidden_two = (normed_two * gain_two).astype(jnp.bfloat16)
    gate = jnp.dot(hidden_two, expand_b[0], preferred_element_type=jnp.float32)
    up = jnp.dot(hidden_two, expand_b[1], preferred_element_type=jnp.float32)
    gelu_value, gelu_slope = gelu_parts(gate)
    inner = (gelu_value * up).astype(jnp.bfloat16)
    block_output = residual + jnp.dot(inner, reduce_b, preferred_element_type=jnp.float32)
    cotangent_b = cotangent.astype(jnp.bfloat16)
    d_inner = against(cotangent_b, reduce_b)
    d_gate = (d_inner * up * gelu_slope).astype(jnp.bfloat16)
    d_up = (d_inner * gelu_value).astype(jnp.bfloat16)
    grad_reduce = contract_rows(inner, cotangent_b)
    grad_expand = jnp.stack([contract_rows(hidden_two, d_gate), contract_rows(hidden_two, d_up)])
    d_hidden_two = against(d_gate, expand_b[0]) + against(d_up, expand_b[1])
    d_residual = cotangent + norm_back(d_hidden_two, normed_two, rstd_two, gain_two)
    grad_feed = lax.optimization_barrier(jnp.sum(d_hidden_two * normed_two, axis=0))
    residual_b = d_residual.astype(jnp.bfloat16)
    d_attended = against(residual_b, merge_b).astype(jnp.bfloat16).reshape(length, HEADS, HD)
    grad_merge = contract_rows(attended_flat, residual_b)
    d_query, d_keys, d_values = attend_back(query, keys, values, attended, totals, d_attended)
    d_pre = jnp.stack([rotate_back(d_query, cosine, sine), rotate_back(d_keys, cosine, sine), d_values])
    d_pre = d_pre.astype(jnp.bfloat16).reshape(3, length, D).astype(jnp.float32)
    grad_triple = jnp.einsum('sd,csf->cdf', hidden_one.astype(jnp.float32), d_pre)
    d_hidden_one = jnp.einsum('csf,cdf->sd', d_pre, triple_b.astype(jnp.float32))
    input_grad = d_residual + norm_back(d_hidden_one, normed_one, rstd_one, gain_one)
    grad_attend = lax.optimization_barrier(jnp.sum(d_hidden_one * normed_one, axis=0))
    new_grads = (grads[0] + grad_attend, grads[1] + grad_triple, grads[2] + grad_merge, grads[3] + grad_feed, grads[4] + grad_expand, grads[5] + grad_reduce)
    return (new_grads, (block_output, input_grad))

def adam_step(weight, first, second, grad, rate):
    first_new = BETA_FIRST * first + (1.0 - BETA_FIRST) * grad
    second_new = BETA_SECOND * second + (1.0 - BETA_SECOND) * grad * grad
    first_hat = first_new / (1.0 - BETA_FIRST ** STEP_COUNT)
    second_hat = second_new / (1.0 - BETA_SECOND ** STEP_COUNT)
    fresh = weight - rate * (first_hat / (jnp.sqrt(second_hat) + ADAM_EPS) + DECAY * weight)
    return (fresh, first_new, second_new)

def reference(block_input, out_cotangent, gain_attend, weight_triple, weight_merge, gain_feed, weight_expand, weight_reduce, mean_attend, mean_triple, mean_merge, mean_feed, mean_expand, mean_reduce, square_attend, square_triple, square_merge, square_feed, square_expand, square_reduce):
    weights = (gain_attend, weight_triple, weight_merge, gain_feed, weight_expand, weight_reduce)
    params = (round_gain(gain_attend), weight_triple.astype(jnp.bfloat16), weight_merge.astype(jnp.bfloat16), round_gain(gain_feed), weight_expand.astype(jnp.bfloat16), weight_reduce.astype(jnp.bfloat16))
    start_grads = tuple((jnp.zeros(item.shape, jnp.float32) for item in weights))
    count_seqs = TOKENS // LEN
    pieces = (block_input.reshape(count_seqs, LEN, D), out_cotangent.reshape(count_seqs, LEN, D))
    grads, (outputs, input_grads) = lax.scan(partial(sequence_pass, params), start_grads, pieces)
    firsts = (mean_attend, mean_triple, mean_merge, mean_feed, mean_expand, mean_reduce)
    seconds = (square_attend, square_triple, square_merge, square_feed, square_expand, square_reduce)
    rates = (RATE_GAIN, RATE_MATRIX, RATE_MATRIX, RATE_GAIN, RATE_MATRIX, RATE_MATRIX)
    stepped = [adam_step(weight, first, second, grad, rate) for weight, first, second, grad, rate in zip(weights, firsts, seconds, grads, rates)]
    fresh = tuple((item[0] for item in stepped))
    first_new = tuple((item[1] for item in stepped))
    second_new = tuple((item[2] for item in stepped))
    return (outputs.reshape(TOKENS, D), input_grads.reshape(TOKENS, D), grads[0], grads[1], grads[2], grads[3], grads[4], grads[5], fresh[0], fresh[1], fresh[2], fresh[3], fresh[4], fresh[5], first_new[0], first_new[1], first_new[2], first_new[3], first_new[4], first_new[5], second_new[0], second_new[1], second_new[2], second_new[3], second_new[4], second_new[5])
```

```python
import math

import jax
import jax.numpy as jnp
import numpy as np
from jax import lax
from jax.experimental import pallas as pl
from jax.experimental.pallas import tpu as pltpu
from jax.sharding import PartitionSpec as P

HD = 64
WINDOW = 128
HALF = WINDOW // 2
TILE = 128
LANES = 128

NORM_EPS = 1e-05
ROPE_BASE = 10000.0
BETA_FIRST = 0.9
BETA_SECOND = 0.999
ADAM_EPS = 1e-08
DECAY = 0.01
RATE_MATRIX = 0.02
RATE_GAIN = 0.2
STEP_COUNT = 3.0
MASKED = -1e30

INTERPRET = False
F32 = jnp.float32
BF16 = jnp.bfloat16


def run_kernel(body, outs, args, scalars=0, scratch=(), name=None):
    in_specs = [pl.BlockSpec(memory_space=pltpu.SMEM)] * scalars
    in_specs += [pl.BlockSpec(memory_space=pltpu.VMEM)] * (len(args) - scalars)
    return pl.pallas_call(
        body,
        out_shape=[jax.ShapeDtypeStruct(shape, kind) for shape, kind in outs],
        in_specs=in_specs,
        out_specs=[pl.BlockSpec(memory_space=pltpu.VMEM)] * len(outs),
        scratch_shapes=list(scratch),
        interpret=INTERPRET,
        name=name,
    )(*args)


def dot_nn(left, right):
    return lax.dot_general(left, right, (((1,), (0,)), ((), ())), preferred_element_type=F32)


def dot_nt(left, right):
    return lax.dot_general(left, right, (((1,), (1,)), ((), ())), preferred_element_type=F32)


def dot_tn(left, right):
    return lax.dot_general(left, right, (((0,), (0,)), ((), ())), preferred_element_type=F32)


def lane_iota(shape):
    return lax.broadcasted_iota(jnp.int32, shape, len(shape) - 1)


def shift(value, amount):
    return pltpu.roll(value, amount, 1)


def rope_tables(length):
    half = HD // 2
    freqs = np.power(np.float64(ROPE_BASE), -2.0 * np.arange(half) / HD)
    angles = np.arange(length)[:, None] * freqs[None, :]
    tile = LANES // half
    return (
        np.tile(np.cos(angles), (1, tile)).astype(np.float32),
        np.tile(np.sin(angles), (1, tile)).astype(np.float32),
    )


def turn(value, cosine, sine, back):
    lanes = lane_iota(value.shape)
    first = (lanes % HD) < HD // 2
    ahead = shift(value, LANES - HD // 2)
    behind = shift(value, HD // 2)
    if back:
        other = jnp.where(first, ahead, -behind)
    else:
        other = jnp.where(first, -ahead, behind)
    return value * cosine + other * sine


def gelu_parts(value):
    normal_share = 0.5 * (1.0 + lax.erf(value * (1.0 / math.sqrt(2.0))))
    density = jnp.exp(-0.5 * value * value) * (1.0 / math.sqrt(2.0 * math.pi))
    return (value * normal_share, normal_share + value * density)


def row_stats(rows):
    center = rows - jnp.mean(rows, axis=-1, keepdims=True)
    scale = lax.rsqrt(jnp.mean(center * center, axis=-1, keepdims=True) + NORM_EPS)
    return center * scale, scale


def scaled_back(scaled, normed, scale):
    return scale * (
        scaled
        - jnp.mean(scaled, axis=-1, keepdims=True)
        - normed * jnp.mean(scaled * normed, axis=-1, keepdims=True)
    )


def at_block(offsets, index, size):
    return pl.ds(pl.multiple_of(offsets[index], size), size)


def tile_mask(start, length):
    row = lax.broadcasted_iota(jnp.int32, (TILE, TILE + WINDOW), 0)
    col = lax.broadcasted_iota(jnp.int32, (TILE, TILE + WINDOW), 1)
    ahead = col - row
    key = col + (start - HALF)
    return (ahead >= 0) & (ahead <= WINDOW) & (key >= 0) & (key < length)


def low_high():
    lanes = lane_iota((1, LANES))
    low = (lanes < HD).astype(F32)
    return low.astype(BF16), (1.0 - low).astype(BF16)


def fill_padded(target, value, length):
    target[0:HALF, :] = jnp.zeros((HALF, LANES), target.dtype)
    target[HALF + length : length + WINDOW, :] = jnp.zeros((HALF, LANES), target.dtype)
    target[HALF : HALF + length, :] = value


def prepare_kernel(rows_ref, cot_ref, out_ref):
    width = rows_ref.shape[1]
    normed, _ = row_stats(rows_ref[...])
    out_ref[:, :width] = normed.astype(BF16)
    out_ref[:, width:] = cot_ref[...].astype(BF16)


def make_attend(length, width, rows, chunks):
    scale = 1.0 / math.sqrt(HD)

    def body(places, spots, cos_ref, sin_ref, *refs):
        blocks, refs = refs[:4], refs[4:]
        parts, refs = refs[:chunks], refs[chunks:]
        normed, cot, weight, qkv, att, lse, keep, send = refs[:8]
        k_pad, k2_pad, v_pad, v2_pad, partial = refs[8:]
        deep = width // chunks
        for j in range(4):
            normed[at_block(places, j, rows), :] = blocks[j][:, :width]
            cot[at_block(places, j, rows), :] = blocks[j][:, width:]
        for s in range(chunks):
            weight[at_block(spots, s, deep), :] = parts[s][...]
        pre = dot_nn(normed[...], weight[:, : 5 * LANES])
        cosine, sine = cos_ref[...], sin_ref[...]
        lanes = lane_iota((length, LANES))
        is_low = lanes < HD
        for t in range(3):
            turned = turn(pre[:, t * LANES : (t + 1) * LANES], cosine, sine, False)
            qkv[:, t * LANES : (t + 1) * LANES] = turned.astype(BF16)
            if t == 1:
                fill_padded(k_pad, turned.astype(BF16), length)
            if t == 2:
                fill_padded(k2_pad, shift(turned, HD).astype(BF16), length)
        v_main = pre[:, 3 * LANES : 4 * LANES].astype(BF16)
        v_rest = jnp.where(is_low, pre[:, 4 * LANES : 5 * LANES], 0.0).astype(BF16)
        qkv[:, 3 * LANES : 4 * LANES] = v_main
        qkv[:, 4 * LANES : 5 * LANES] = v_rest
        fill_padded(v_pad, v_main, length)
        fill_padded(v2_pad, v_rest, length)
        low, high = low_high()
        tile_lanes = lane_iota((TILE, LANES))
        tile_low = tile_lanes < HD
        for t in range(length // TILE):
            span = slice(t * TILE, (t + 1) * TILE)
            window = slice(t * TILE, (t + 1) * TILE + WINDOW)
            mask = tile_mask(t * TILE, length)
            q_main, q_rest = qkv[span, 0:LANES], qkv[span, 2 * LANES : 3 * LANES]
            found, totals = [], []
            for q, k_ref, v_ref in (
                (q_main * low, k_pad, v_pad),
                (q_main * high, k_pad, v_pad),
                (q_rest * low, k2_pad, v2_pad),
            ):
                score = jnp.where(mask, dot_nt(q, k_ref[window, :]) * scale, MASKED)
                top = jnp.max(score, axis=-1, keepdims=True)
                total = top + jnp.log(jnp.sum(jnp.exp(score - top), axis=-1, keepdims=True))
                probs = jnp.exp(score - total).astype(BF16)
                found.append(dot_nn(probs, v_ref[window, :]))
                totals.append(total)
            main = jnp.where(tile_low, found[0], found[1])
            rest = shift(jnp.where(tile_low, found[2], 0.0), HD)
            att[span, 0:LANES] = rest.astype(BF16)
            att[span, LANES : 2 * LANES] = main.astype(BF16)
            lse[span, :] = jnp.where(
                tile_lanes == 0, totals[0], jnp.where(tile_lanes == 1, totals[1], totals[2])
            )
        partial[...] = dot_nt(att[...], weight[:, 4 * LANES :])
        for i, j in enumerate((0, 2)):
            keep[i] = partial[at_block(places, j, rows), :]
        for i, j in enumerate((1, 3)):
            send[i] = partial[at_block(places, j, rows), :].astype(BF16)

    return body


def core_sum_kernel(keep_ref, got_ref, mine_ref, send_ref):
    mine_ref[...] = keep_ref[0] + got_ref[0].astype(F32)
    send_ref[...] = (keep_ref[1] + got_ref[1].astype(F32)).astype(BF16)


def second_norm_kernel(rows_ref, mine_ref, got_ref, residual_ref, normed_ref):
    residual = rows_ref[...] + mine_ref[...] + got_ref[...].astype(F32)
    residual_ref[...] = residual
    normed, _ = row_stats(residual)
    normed_ref[...] = normed.astype(BF16)


def make_feed(length, width, rows, chunks):
    def body(places, spots, *refs):
        blocks, refs = refs[:4], refs[4:]
        cot, refs = refs[0], refs[1:]
        parts, refs = refs[:chunks], refs[chunks:]
        normed, d_all, inner_all, keep_s, send_s, keep_o, send_o = refs[:7]
        weight, partial = refs[7:]
        deep = width // chunks
        for j in range(4):
            normed[at_block(places, j, rows), :] = blocks[j][...]
        for s in range(chunks):
            weight[at_block(spots, s, deep), :] = parts[s][...]
        both = dot_nn(normed[...], weight[:, : 5 * LANES])
        d_inner = dot_nn(cot[...], weight[:, 4 * LANES :])
        lanes = lane_iota((length, LANES))
        valid = lanes < LANES // 4
        for t in range(3):
            if t < 2:
                gate = both[:, t * LANES : (t + 1) * LANES]
                up = both[:, (2 + t) * LANES : (3 + t) * LANES]
                slope_in = d_inner[:, (1 + t) * LANES : (2 + t) * LANES]
            else:
                gate = both[:, 4 * LANES : 5 * LANES]
                up = shift(gate, LANES - LANES // 4)
                slope_in = shift(d_inner[:, 0:LANES], LANES // 2)
            value, slope = gelu_parts(gate)
            inner = value * up
            d_gate = slope_in * up * slope
            d_up = slope_in * value
            if t < 2:
                inner_all[:, (1 + t) * LANES : (2 + t) * LANES] = inner.astype(BF16)
                d_all[:, t * LANES : (t + 1) * LANES] = d_gate.astype(BF16)
                d_all[:, (2 + t) * LANES : (3 + t) * LANES] = d_up.astype(BF16)
            else:
                inner_all[:, 0:LANES] = shift(
                    jnp.where(valid, inner, 0.0), LANES // 2
                ).astype(BF16)
                d_all[:, 4 * LANES : 5 * LANES] = jnp.where(
                    valid, d_gate, shift(jnp.where(valid, d_up, 0.0), LANES // 4)
                ).astype(BF16)
        partial[...] = dot_nt(d_all[...], weight[:, : 5 * LANES])
        for i, j in enumerate((0, 2)):
            keep_s[i] = partial[at_block(places, j, rows), :]
        for i, j in enumerate((1, 3)):
            send_s[i] = partial[at_block(places, j, rows), :].astype(BF16)
        partial[...] = dot_nt(inner_all[...], weight[:, 4 * LANES :])
        for i, j in enumerate((0, 2)):
            keep_o[i] = partial[at_block(places, j, rows), :]
        for i, j in enumerate((1, 3)):
            send_o[i] = partial[at_block(places, j, rows), :].astype(BF16)

    return body


def spread_chunks(grad, spots, outs, deep):
    outs[0][...] = grad[at_block(spots, 0, deep), :]
    for s in range(1, len(outs)):
        outs[s][...] = grad[at_block(spots, s, deep), :].astype(BF16)


def make_feed_grads(chunks):
    def body(spots, normed, cot, d_all, inner_all, *refs):
        outs, grad = refs[:chunks], refs[chunks]
        expand = dot_tn(normed[...], d_all[...])
        reduce = dot_tn(cot[...], inner_all[...])
        grad[:, : 4 * LANES] = expand[:, : 4 * LANES]
        grad[:, 4 * LANES : 5 * LANES] = expand[:, 4 * LANES :] + reduce[:, :LANES]
        grad[:, 5 * LANES :] = reduce[:, LANES:]
        spread_chunks(grad, spots, outs, grad.shape[0] // chunks)

    return body


def residual_back_kernel(cot_ref, residual_ref, mine_ref, got_ref, grad_ref, send_ref):
    normed, scale = row_stats(residual_ref[...])
    scaled = mine_ref[...] + got_ref[...].astype(F32)
    grad = cot_ref[...] + scaled_back(scaled, normed, scale)
    grad_ref[...] = grad
    send_ref[...] = grad.astype(BF16)


def make_attend_back(length, width, rows, chunks):
    scale = 1.0 / math.sqrt(HD)

    def body(places, spots, cos_ref, sin_ref, *refs):
        blocks, refs = refs[:4], refs[4:]
        normed, weight, qkv, att, lse = refs[:5]
        d_pre = refs[5]
        outs = refs[6 : 6 + chunks]
        resid, grad, k_pad, k2_pad, v_pad, v2_pad, da, dk, dk2, dv, dv2 = refs[6 + chunks :]
        for j in range(4):
            resid[at_block(places, j, rows), :] = blocks[j][...]
        back = dot_nn(resid[...], weight[:, 4 * LANES :])
        lanes = lane_iota((length, LANES))
        is_low = lanes < HD
        da[:, LANES:] = back[:, LANES:].astype(BF16)
        da[:, :LANES] = shift(jnp.where(is_low, 0.0, back[:, :LANES]), HD).astype(BF16)
        fill_padded(k_pad, qkv[:, LANES : 2 * LANES], length)
        fill_padded(
            k2_pad, shift(qkv[:, 2 * LANES : 3 * LANES].astype(F32), HD).astype(BF16), length
        )
        fill_padded(v_pad, qkv[:, 3 * LANES : 4 * LANES], length)
        fill_padded(v2_pad, qkv[:, 4 * LANES : 5 * LANES], length)
        for piece in (dk, dk2, dv, dv2):
            piece[...] = jnp.zeros_like(piece)
        low, high = low_high()
        tile_low = lane_iota((TILE, LANES)) < HD
        cosine, sine = cos_ref[...], sin_ref[...]
        for t in range(length // TILE):
            span = slice(t * TILE, (t + 1) * TILE)
            window = slice(t * TILE, (t + 1) * TILE + WINDOW)
            mask = tile_mask(t * TILE, length)
            q_main, q_rest = qkv[span, 0:LANES], qkv[span, 2 * LANES : 3 * LANES]
            da_main, da_rest = da[span, LANES:], da[span, :LANES]
            main = da_main.astype(F32) * att[span, LANES:].astype(F32)
            rest = da_rest.astype(F32) * shift(att[span, :LANES].astype(F32), HD)
            deltas = (
                jnp.sum(jnp.where(tile_low, main, 0.0), axis=-1, keepdims=True),
                jnp.sum(jnp.where(tile_low, 0.0, main), axis=-1, keepdims=True),
                jnp.sum(jnp.where(tile_low, rest, 0.0), axis=-1, keepdims=True),
            )
            d_query = []
            for h, (q, d, k_ref, v_ref, dk_ref, dv_ref) in enumerate(
                (
                    (q_main * low, da_main * low, k_pad, v_pad, dk, dv),
                    (q_main * high, da_main * high, k_pad, v_pad, dk, dv),
                    (q_rest * low, da_rest * low, k2_pad, v2_pad, dk2, dv2),
                )
            ):
                keys = k_ref[window, :]
                score = jnp.where(mask, dot_nt(q, keys) * scale, MASKED)
                probs = jnp.exp(score - lse[span, h : h + 1])
                d_probs = dot_nt(d, v_ref[window, :])
                d_score = (probs * (d_probs - deltas[h]) * scale).astype(BF16)
                d_query.append(dot_nn(d_score, keys))
                dk_ref[window, :] += dot_tn(d_score, q)
                dv_ref[window, :] += dot_tn(probs.astype(BF16), d)
            d_main = jnp.where(tile_low, d_query[0], d_query[1])
            d_pre[span, 0:LANES] = turn(d_main, cosine[span], sine[span], True).astype(BF16)
            grad[span, 0:LANES] = jnp.where(tile_low, d_query[2], 0.0)
        inside = slice(HALF, HALF + length)
        d_pre[:, LANES : 2 * LANES] = turn(dk[inside, :], cosine, sine, True).astype(BF16)
        rest = jnp.where(is_low, grad[0:length, 0:LANES], shift(dk2[inside, :], HD))
        d_pre[:, 2 * LANES : 3 * LANES] = turn(rest, cosine, sine, True).astype(BF16)
        d_pre[:, 3 * LANES : 4 * LANES] = dv[inside, :].astype(BF16)
        d_pre[:, 4 * LANES : 5 * LANES] = dv2[inside, :].astype(BF16)
        triple = dot_tn(normed[...], d_pre[...])
        merge = dot_tn(resid[...], att[...])
        grad[:, : 4 * LANES] = triple[:, : 4 * LANES]
        grad[:, 4 * LANES : 5 * LANES] = triple[:, 4 * LANES :] + merge[:, :LANES]
        grad[:, 5 * LANES :] = merge[:, LANES:]
        spread_chunks(grad, spots, outs, width // chunks)

    return body


def make_input_share(rows):
    def body(places, d_pre, weight, keep, send, partial):
        partial[...] = dot_nt(d_pre[...], weight[:, : 5 * LANES])
        for i, j in enumerate((0, 2)):
            keep[i] = partial[at_block(places, j, rows), :]
        for i, j in enumerate((1, 3)):
            send[i] = partial[at_block(places, j, rows), :].astype(BF16)

    return body


def finish_kernel(
    rows_ref, d_residual_ref, mine_ref, got_ref, residual_ref, out_mine, out_got, grad_ref, out_ref
):
    normed, scale = row_stats(rows_ref[...])
    scaled = mine_ref[...] + got_ref[...].astype(F32)
    grad_ref[...] = d_residual_ref[...] + scaled_back(scaled, normed, scale)
    out_ref[...] = residual_ref[...] + out_mine[...] + out_got[...].astype(F32)


def adam_step(weight, first, second, grad, rate):
    first_new = BETA_FIRST * first + (1.0 - BETA_FIRST) * grad
    second_new = BETA_SECOND * second + (1.0 - BETA_SECOND) * grad * grad
    first_hat = first_new / (1.0 - BETA_FIRST**STEP_COUNT)
    second_hat = second_new / (1.0 - BETA_SECOND**STEP_COUNT)
    fresh = weight - rate * (first_hat / (jnp.sqrt(second_hat) + ADAM_EPS) + DECAY * weight)
    return (fresh, first_new, second_new)


def pack_attend(gain, triple, merge):
    folded = (gain.astype(BF16).astype(F32)[:, None] * triple.astype(BF16).astype(F32)).astype(BF16)
    turned = merge.astype(BF16).T
    q, k, v = folded[0], folded[1], folded[2]
    return jnp.concatenate(
        [
            q[:, :LANES],
            k[:, :LANES],
            q[:, LANES:],
            k[:, LANES:],
            v[:, :LANES],
            v[:, LANES:],
            turned[:, LANES:],
            turned[:, :LANES],
        ],
        axis=1,
    )


def unpack_attend(pack, gain):
    scale = gain.astype(BF16).astype(F32)[:, None]
    q = jnp.concatenate([pack[:, :LANES], pack[:, 2 * LANES : 2 * LANES + HD]], axis=1)
    k = jnp.concatenate([pack[:, LANES : 2 * LANES], pack[:, 2 * LANES + HD : 3 * LANES]], axis=1)
    v = jnp.concatenate([pack[:, 3 * LANES : 4 * LANES], pack[:, 4 * LANES : 4 * LANES + HD]], axis=1)
    plain = jnp.stack([q, k, v])
    merge = jnp.concatenate([pack[:, 5 * LANES :], pack[:, 4 * LANES + HD : 5 * LANES]], axis=1).T
    return plain, plain * scale, merge


def pack_feed(gain, expand, reduce):
    folded = (gain.astype(BF16).astype(F32)[:, None] * expand.astype(BF16).astype(F32)).astype(BF16)
    turned = reduce.astype(BF16).T
    wide = 2 * LANES
    spare = jnp.zeros((turned.shape[0], LANES // 4), BF16)
    return jnp.concatenate(
        [
            folded[0][:, :wide],
            folded[1][:, :wide],
            folded[0][:, wide:],
            folded[1][:, wide:],
            turned[:, wide:],
            spare,
            turned[:, :wide],
        ],
        axis=1,
    )


def unpack_feed(pack, gain):
    scale = gain.astype(BF16).astype(F32)[:, None]
    wide, part = 2 * LANES, LANES // 4
    rest = pack[:, 4 * LANES : 5 * LANES]
    one = jnp.concatenate([pack[:, :wide], rest[:, :part]], axis=1)
    two = jnp.concatenate([pack[:, wide : 2 * wide], rest[:, part : 2 * part]], axis=1)
    plain = jnp.stack([one, two])
    reduce = jnp.concatenate([pack[:, 5 * LANES :], rest[:, 2 * part : 3 * part]], axis=1).T
    return plain, plain * scale, reduce


def make_on_device(sizes):
    dp, mp = sizes["dp"], sizes["mp"]
    direct = dp == 8

    def over_mp(value, step):
        return lax.ppermute(value, "mp", [(i, i ^ step) for i in range(mp)])

    def over_dp(value, step):
        return lax.ppermute(value, "dp", [(i, i ^ step) for i in range(dp)])

    def gather_chunks(shard):
        if not direct:
            return [lax.all_gather(shard, "dp", axis=0, tiled=True)]
        along = [shard] + [over_dp(shard, s) for s in (2, 4, 6)]
        across = [over_dp(piece, 1) for piece in along]
        return [piece for pair in zip(along, across) for piece in pair]

    def reduce_chunks(chunks):
        if not direct:
            return lax.psum_scatter(chunks[0], "dp", scatter_dimension=0, tiled=True)
        total = chunks[0]
        for s in range(1, dp):
            total = total + over_dp(chunks[s], s).astype(F32)
        return total

    def on_device(
        block_input,
        out_cotangent,
        gain_attend,
        weight_triple,
        weight_merge,
        gain_feed,
        weight_expand,
        weight_reduce,
        *moments,
    ):
        rows, width = block_input.shape
        length = rows * mp
        chunks = dp if direct else 1
        deep = width // chunks
        me, here = lax.axis_index("mp"), lax.axis_index("dp")
        places = jnp.bitwise_xor(me, jnp.arange(4, dtype=jnp.int32)) * rows
        if direct:
            spots = jnp.bitwise_xor(here, jnp.arange(dp, dtype=jnp.int32)) * deep
        else:
            spots = jnp.zeros((1,), jnp.int32)
        cosine, sine = (jnp.asarray(table) for table in rope_tables(length))

        first_pack = pack_attend(gain_attend, weight_triple, weight_merge)
        second_pack = pack_feed(gain_feed, weight_expand, weight_reduce)
        (own,) = run_kernel(
            prepare_kernel, [((rows, 2 * width), BF16)], (block_input, out_cotangent), name="prepare"
        )
        first_chunks = gather_chunks(first_pack)
        far = over_mp(own, 2)
        blocks = [own, over_mp(own, 1), far, over_mp(far, 1)]
        second_chunks = gather_chunks(second_pack)

        half_rows = (2, rows, width)
        pad = length + WINDOW
        normed, cot, weight, qkv, att, lse, keep, send = run_kernel(
            make_attend(length, width, rows, chunks),
            [
                ((length, width), BF16),
                ((length, width), BF16),
                ((width, 6 * LANES), BF16),
                ((length, 5 * LANES), BF16),
                ((length, 2 * LANES), BF16),
                ((length, LANES), F32),
                (half_rows, F32),
                (half_rows, BF16),
            ],
            (places, spots, cosine, sine, *blocks, *first_chunks),
            scalars=2,
            scratch=[pltpu.VMEM((pad, LANES), BF16)] * 4 + [pltpu.VMEM((length, width), F32)],
            name="attend",
        )

        def to_owner(keep, send, name):
            mine, far = run_kernel(
                core_sum_kernel,
                [((rows, width), F32), ((rows, width), BF16)],
                (keep, over_mp(send, 1)),
                name=name,
            )
            return mine, over_mp(far, 2)

        mine, got = to_owner(keep, send, "merge_sum")
        residual, normed_two = run_kernel(
            second_norm_kernel,
            [((rows, width), F32), ((rows, width), BF16)],
            (block_input, mine, got),
            name="second_norm",
        )
        far = over_mp(normed_two, 2)
        blocks = [normed_two, over_mp(normed_two, 1), far, over_mp(far, 1)]
        normed_two_all, d_all, inner_all, keep_s, send_s, keep_o, send_o = run_kernel(
            make_feed(length, width, rows, chunks),
            [
                ((length, width), BF16),
                ((length, 5 * LANES), BF16),
                ((length, 3 * LANES), BF16),
                (half_rows, F32),
                (half_rows, BF16),
                (half_rows, F32),
                (half_rows, BF16),
            ],
            (places, spots, *blocks, cot, *second_chunks),
            scalars=2,
            scratch=[pltpu.VMEM((width, 7 * LANES), BF16), pltpu.VMEM((length, width), F32)],
            name="feed",
        )
        mine, got = to_owner(keep_s, send_s, "feed_sum")
        out_mine, out_got = to_owner(keep_o, send_o, "out_sum")
        kinds = [F32] + [BF16] * (chunks - 1)
        feed_chunks = run_kernel(
            make_feed_grads(chunks),
            [((deep, 7 * LANES), kind) for kind in kinds],
            (spots, normed_two_all, cot, d_all, inner_all),
            scalars=1,
            scratch=[pltpu.VMEM((width, 7 * LANES), F32)],
            name="feed_grads",
        )
        d_residual, residual_b = run_kernel(
            residual_back_kernel,
            [((rows, width), F32), ((rows, width), BF16)],
            (out_cotangent, residual, mine, got),
            name="residual_back",
        )
        far = over_mp(residual_b, 2)
        blocks = [residual_b, over_mp(residual_b, 1), far, over_mp(far, 1)]
        feed_sum = reduce_chunks(feed_chunks)
        d_pre, *attend_chunks = run_kernel(
            make_attend_back(length, width, rows, chunks),
            [((length, 5 * LANES), BF16)] + [((deep, 6 * LANES), kind) for kind in kinds],
            (places, spots, cosine, sine, *blocks, normed, weight, qkv, att, lse),
            scalars=2,
            scratch=[
                pltpu.VMEM((length, width), BF16),
                pltpu.VMEM((width, 6 * LANES), F32),
            ]
            + [pltpu.VMEM((pad, LANES), BF16)] * 4
            + [pltpu.VMEM((length, 2 * LANES), BF16)]
            + [pltpu.VMEM((pad, LANES), F32)] * 4,
            name="attend_back",
        )
        attend_sum = reduce_chunks(attend_chunks)
        keep, send = run_kernel(
            make_input_share(rows),
            [(half_rows, F32), (half_rows, BF16)],
            (places, d_pre, weight),
            scalars=1,
            scratch=[pltpu.VMEM((length, width), F32)],
            name="input_share",
        )
        mine, got = to_owner(keep, send, "input_sum")
        input_grad, block_output = run_kernel(
            finish_kernel,
            [((rows, width), F32), ((rows, width), F32)],
            (block_input, d_residual, mine, got, residual, out_mine, out_got),
            name="finish",
        )

        plain_triple, grad_triple, grad_merge = unpack_attend(attend_sum, gain_attend)
        plain_expand, grad_expand, grad_reduce = unpack_feed(feed_sum, gain_feed)
        share_attend = jnp.sum(plain_triple * weight_triple.astype(BF16).astype(F32), axis=(0, 2))
        share_feed = jnp.sum(plain_expand * weight_expand.astype(BF16).astype(F32), axis=(0, 2))

        def over_parts(share):
            if not direct:
                return lax.psum(share, "mp")
            share = share + over_mp(share, 1)
            return share + over_mp(share, 2)

        grads = (
            over_parts(share_attend),
            grad_triple,
            grad_merge,
            over_parts(share_feed),
            grad_expand,
            grad_reduce,
        )
        weights = (gain_attend, weight_triple, weight_merge, gain_feed, weight_expand, weight_reduce)
        rates = (RATE_GAIN, RATE_MATRIX, RATE_MATRIX, RATE_GAIN, RATE_MATRIX, RATE_MATRIX)
        stepped = [
            adam_step(weight, first, second, grad, rate)
            for weight, first, second, grad, rate in zip(
                weights, moments[:6], moments[6:], grads, rates
            )
        ]
        fresh = tuple(item[0] for item in stepped)
        first_new = tuple(item[1] for item in stepped)
        second_new = tuple(item[2] for item in stepped)
        return (block_output, input_grad) + grads + fresh + first_new + second_new

    return on_device


def solution(mesh):
    rows = P(("dp", "mp"), None)
    params = (P("dp"), P(None, "dp", "mp"), P("mp", "dp"), P("dp"), P(None, "dp", "mp"), P("mp", "dp"))
    return jax.shard_map(
        make_on_device(dict(mesh.shape)),
        mesh=mesh,
        in_specs=(rows, rows) + params * 3,
        out_specs=(rows, rows) + params * 4,
        check_vma=False,
    )
```

```python
import math

import jax
import jax.numpy as jnp
import numpy as np
from jax import lax
from jax.experimental import pallas as pl
from jax.experimental.pallas import tpu as pltpu
from jax.sharding import PartitionSpec as P


HD = 64
WINDOW = 128
HALF = WINDOW // 2
TILE = 128
LANES = 128

NORM_EPS = 1e-05
ROPE_BASE = 10000.0
BETA_FIRST = 0.9
BETA_SECOND = 0.999
ADAM_EPS = 1e-08
DECAY = 0.01
RATE_MATRIX = 0.02
RATE_GAIN = 0.2
STEP_COUNT = 3.0
MASKED = -1e30

INTERPRET = False
F32 = jnp.float32
BF16 = jnp.bfloat16


def run_kernel(body, outs, args, scalars=0, scratch=(), limit=24, final=False):
    in_specs = [pl.BlockSpec(memory_space=pltpu.SMEM)] * scalars
    in_specs += [pl.BlockSpec(memory_space=pltpu.VMEM)] * (len(args) - scalars)
    out_shape = [jax.ShapeDtypeStruct(shape, kind) for shape, kind in outs]
    if not INTERPRET:
        args = args[:scalars] + tuple(
            pltpu.with_memory_space_constraint(item, pltpu.VMEM) for item in args[scalars:]
        )
        if not final:
            out_shape = [pltpu.VMEM(shape, kind) for shape, kind in outs]
    return pl.pallas_call(
        body,
        out_shape=out_shape,
        in_specs=in_specs,
        out_specs=[pl.BlockSpec(memory_space=pltpu.VMEM)] * len(outs),
        scratch_shapes=list(scratch),
        interpret=INTERPRET,
        compiler_params=pltpu.CompilerParams(vmem_limit_bytes=limit << 20),
    )(*args)


def dot_nn(left, right):
    return lax.dot_general(left, right, (((1,), (0,)), ((), ())), preferred_element_type=F32)


def dot_nt(left, right):
    return lax.dot_general(left, right, (((1,), (1,)), ((), ())), preferred_element_type=F32)


def dot_tn(left, right):
    return lax.dot_general(left, right, (((0,), (0,)), ((), ())), preferred_element_type=F32)


def lane_iota(shape):
    return lax.broadcasted_iota(jnp.int32, shape, len(shape) - 1)


def shift(value, amount):
    return pltpu.roll(value, amount, 1)


def rope_tables(length):
    half = HD // 2
    freqs = np.power(np.float64(ROPE_BASE), -2.0 * np.arange(half) / HD)
    angles = np.arange(length)[:, None] * freqs[None, :]
    tile = LANES // half
    return (
        np.tile(np.cos(angles), (1, tile)).astype(np.float32),
        np.tile(np.sin(angles), (1, tile)).astype(np.float32),
    )


def turn(value, cosine, sine, back):
    lanes = lane_iota(value.shape)
    first = (lanes % HD) < HD // 2
    ahead = shift(value, LANES - HD // 2)
    behind = shift(value, HD // 2)
    if back:
        other = jnp.where(first, ahead, -behind)
    else:
        other = jnp.where(first, -ahead, behind)
    return value * cosine + other * sine


def gelu_parts(value):
    normal_share = 0.5 * (1.0 + lax.erf(value * (1.0 / math.sqrt(2.0))))
    density = jnp.exp(-0.5 * value * value) * (1.0 / math.sqrt(2.0 * math.pi))
    return (value * normal_share, normal_share + value * density)


def row_stats(rows):
    center = rows - jnp.mean(rows, axis=-1, keepdims=True)
    scale = lax.rsqrt(jnp.mean(center * center, axis=-1, keepdims=True) + NORM_EPS)
    return center * scale, scale


def scaled_back(scaled, normed, scale):
    return scale * (
        scaled
        - jnp.mean(scaled, axis=-1, keepdims=True)
        - normed * jnp.mean(scaled * normed, axis=-1, keepdims=True)
    )


def at_block(offsets, index, size):
    return pl.ds(pl.multiple_of(offsets[index], size), size)


def tile_mask(start, length):
    row = lax.broadcasted_iota(jnp.int32, (TILE, TILE + WINDOW), 0)
    col = lax.broadcasted_iota(jnp.int32, (TILE, TILE + WINDOW), 1)
    ahead = col - row
    key = col + (start - HALF)
    return (ahead >= 0) & (ahead <= WINDOW) & (key >= 0) & (key < length)


def low_high():
    lanes = lane_iota((1, LANES))
    low = (lanes < HD).astype(F32)
    return low.astype(BF16), (1.0 - low).astype(BF16)


def fill_padded(target, value, length):
    target[0:HALF, :] = jnp.zeros((HALF, LANES), target.dtype)
    target[HALF + length : length + WINDOW, :] = jnp.zeros((HALF, LANES), target.dtype)
    target[HALF : HALF + length, :] = value


def prepare_kernel(places, spots, rows_ref, cot_ref, out_ref):
    width = rows_ref.shape[1]
    normed, _ = row_stats(rows_ref[...])
    out_ref[:, :width] = normed.astype(BF16)
    out_ref[:, width:] = cot_ref[...].astype(BF16)


def make_attend(length, width, rows, chunks):
    scale = 1.0 / math.sqrt(HD)

    def body(places, spots, cos_ref, sin_ref, *refs):
        blocks, refs = refs[:4], refs[4:]
        parts, refs = refs[:chunks], refs[chunks:]
        normed, cot, weight, qkv, att, lse, keep, send = refs[:8]
        k_pad, k2_pad, v_pad, v2_pad, partial = refs[8:]
        deep = width // chunks
        for j in range(4):
            normed[at_block(places, j, rows), :] = blocks[j][:, :width]
            cot[at_block(places, j, rows), :] = blocks[j][:, width:]
        for s in range(chunks):
            weight[at_block(spots, s, deep), :] = parts[s][...]
        pre = dot_nn(normed[...], weight[:, : 5 * LANES])
        cosine, sine = cos_ref[...], sin_ref[...]
        lanes = lane_iota((length, LANES))
        is_low = lanes < HD
        for t in range(3):
            turned = turn(pre[:, t * LANES : (t + 1) * LANES], cosine, sine, False)
            qkv[:, t * LANES : (t + 1) * LANES] = turned.astype(BF16)
            if t == 1:
                fill_padded(k_pad, turned.astype(BF16), length)
            if t == 2:
                fill_padded(k2_pad, shift(turned, HD).astype(BF16), length)
        v_main = pre[:, 3 * LANES : 4 * LANES].astype(BF16)
        v_rest = jnp.where(is_low, pre[:, 4 * LANES : 5 * LANES], 0.0).astype(BF16)
        qkv[:, 3 * LANES : 4 * LANES] = v_main
        qkv[:, 4 * LANES : 5 * LANES] = v_rest
        fill_padded(v_pad, v_main, length)
        fill_padded(v2_pad, v_rest, length)
        low, high = low_high()
        tile_lanes = lane_iota((TILE, LANES))
        tile_low = tile_lanes < HD
        for t in range(length // TILE):
            span = slice(t * TILE, (t + 1) * TILE)
            window = slice(t * TILE, (t + 1) * TILE + WINDOW)
            mask = tile_mask(t * TILE, length)
            q_main, q_rest = qkv[span, 0:LANES], qkv[span, 2 * LANES : 3 * LANES]
            found, totals = [], []
            for q, k_ref, v_ref in (
                (q_main * low, k_pad, v_pad),
                (q_main * high, k_pad, v_pad),
                (q_rest * low, k2_pad, v2_pad),
            ):
                score = jnp.where(mask, dot_nt(q, k_ref[window, :]) * scale, MASKED)
                top = jnp.max(score, axis=-1, keepdims=True)
                total = top + jnp.log(jnp.sum(jnp.exp(score - top), axis=-1, keepdims=True))
                probs = jnp.exp(score - total).astype(BF16)
                found.append(dot_nn(probs, v_ref[window, :]))
                totals.append(total)
            main = jnp.where(tile_low, found[0], found[1])
            rest = shift(jnp.where(tile_low, found[2], 0.0), HD)
            att[span, 0:LANES] = rest.astype(BF16)
            att[span, LANES : 2 * LANES] = main.astype(BF16)
            lse[span, :] = jnp.where(
                tile_lanes == 0, totals[0], jnp.where(tile_lanes == 1, totals[1], totals[2])
            )
        partial[...] = dot_nt(att[...], weight[:, 4 * LANES :])
        for i, j in enumerate((0, 2)):
            keep[i] = partial[at_block(places, j, rows), :]
        for i, j in enumerate((1, 3)):
            send[i] = partial[at_block(places, j, rows), :].astype(BF16)

    return body


def core_sum_kernel(keep_ref, got_ref, mine_ref, send_ref):
    mine_ref[...] = keep_ref[0] + got_ref[0].astype(F32)
    send_ref[...] = (keep_ref[1] + got_ref[1].astype(F32)).astype(BF16)


def second_norm_kernel(rows_ref, mine_ref, got_ref, residual_ref, normed_ref):
    residual = rows_ref[...] + mine_ref[...] + got_ref[...].astype(F32)
    residual_ref[...] = residual
    normed, _ = row_stats(residual)
    normed_ref[...] = normed.astype(BF16)


def make_feed(length, width, rows, chunks):
    def body(places, spots, *refs):
        blocks, refs = refs[:4], refs[4:]
        cot, refs = refs[0], refs[1:]
        parts, refs = refs[:chunks], refs[chunks:]
        normed, d_all, inner_all, keep_s, send_s, keep_o, send_o = refs[:7]
        weight, partial = refs[7:]
        deep = width // chunks
        for j in range(4):
            normed[at_block(places, j, rows), :] = blocks[j][...]
        for s in range(chunks):
            weight[at_block(spots, s, deep), :] = parts[s][...]
        both = dot_nn(normed[...], weight[:, : 5 * LANES])
        d_inner = dot_nn(cot[...], weight[:, 4 * LANES :])
        lanes = lane_iota((length, LANES))
        valid = lanes < LANES // 4
        for t in range(3):
            if t < 2:
                gate = both[:, t * LANES : (t + 1) * LANES]
                up = both[:, (2 + t) * LANES : (3 + t) * LANES]
                slope_in = d_inner[:, (1 + t) * LANES : (2 + t) * LANES]
            else:
                gate = both[:, 4 * LANES : 5 * LANES]
                up = shift(gate, LANES - LANES // 4)
                slope_in = shift(d_inner[:, 0:LANES], LANES // 2)
            value, slope = gelu_parts(gate)
            inner = value * up
            d_gate = slope_in * up * slope
            d_up = slope_in * value
            if t < 2:
                inner_all[:, (1 + t) * LANES : (2 + t) * LANES] = inner.astype(BF16)
                d_all[:, t * LANES : (t + 1) * LANES] = d_gate.astype(BF16)
                d_all[:, (2 + t) * LANES : (3 + t) * LANES] = d_up.astype(BF16)
            else:
                inner_all[:, 0:LANES] = shift(
                    jnp.where(valid, inner, 0.0), LANES // 2
                ).astype(BF16)
                d_all[:, 4 * LANES : 5 * LANES] = jnp.where(
                    valid, d_gate, shift(jnp.where(valid, d_up, 0.0), LANES // 4)
                ).astype(BF16)
        partial[...] = dot_nt(d_all[...], weight[:, : 5 * LANES])
        for i, j in enumerate((0, 2)):
            keep_s[i] = partial[at_block(places, j, rows), :]
        for i, j in enumerate((1, 3)):
            send_s[i] = partial[at_block(places, j, rows), :].astype(BF16)
        partial[...] = dot_nt(inner_all[...], weight[:, 4 * LANES :])
        for i, j in enumerate((0, 2)):
            keep_o[i] = partial[at_block(places, j, rows), :]
        for i, j in enumerate((1, 3)):
            send_o[i] = partial[at_block(places, j, rows), :].astype(BF16)

    return body


def spread_chunks(grad, spots, outs, deep, chunks):
    if chunks == 1:
        outs[0][...] = grad[...]
        return
    group = outs[0].shape[0]
    for i in range(chunks // 2):
        mine, send = outs[2 * (i // group)], outs[2 * (i // group) + 1]
        mine[i % group] = grad[at_block(spots, 2 * i, deep), :]
        send[i % group] = grad[at_block(spots, 2 * i + 1, deep), :].astype(BF16)


def chunk_outs(chunks, deep, lanes, groups):
    if chunks == 1:
        return [((deep, lanes), F32)]
    shape = (chunks // 2 // groups, deep, lanes)
    return [(shape, F32), (shape, BF16)] * groups


def chunk_sum_kernel(mine_ref, got_ref, *outs):
    for i, out in enumerate(outs):
        out[...] = (mine_ref[i] + got_ref[i].astype(F32)).astype(out.dtype)


def spread_pairs(grad, spots, outs, deep, chunks):
    if chunks == 1:
        outs[0][...] = grad[...]
        return
    for i, out in enumerate(outs[:-2]):
        for side in range(2):
            out[side] = grad[at_block(spots, 2 * i + side, deep), :].astype(out.dtype)
    outs[-2][...] = grad[at_block(spots, chunks - 2, deep), :]
    outs[-1][...] = grad[at_block(spots, chunks - 1, deep), :].astype(BF16)


def pair_outs(chunks, deep, lanes):
    if chunks == 1:
        return [((deep, lanes), F32)]
    pairs = [((2, deep, lanes), BF16 if i else F32) for i in range(chunks // 2 - 1)]
    return pairs + [((deep, lanes), F32), ((deep, lanes), BF16)]


def near_sum_kernel(mine, got, out):
    out[...] = (mine[...] + got[...].astype(F32)).astype(out.dtype)


def pair_sum_kernel(*refs):
    parts, (mine, send) = refs[:-2], refs[-2:]
    for side, out in enumerate((mine, send)):
        total = parts[0][side]
        for part in parts[1:]:
            total = total + part[side].astype(F32)
        out[...] = total.astype(out.dtype)


def make_feed_grads(chunks):
    def body(spots, normed, cot, d_all, inner_all, *refs):
        outs, grad = refs[:-1], refs[-1]
        expand = dot_tn(normed[...], d_all[...])
        reduce = dot_tn(cot[...], inner_all[...])
        grad[:, : 4 * LANES] = expand[:, : 4 * LANES]
        grad[:, 4 * LANES : 5 * LANES] = expand[:, 4 * LANES :] + reduce[:, :LANES]
        grad[:, 5 * LANES :] = reduce[:, LANES:]
        spread_pairs(grad, spots, outs, grad.shape[0] // chunks, chunks)

    return body


def residual_back_kernel(cot_ref, residual_ref, mine_ref, got_ref, grad_ref, send_ref):
    normed, scale = row_stats(residual_ref[...])
    scaled = mine_ref[...] + got_ref[...].astype(F32)
    grad = cot_ref[...] + scaled_back(scaled, normed, scale)
    grad_ref[...] = grad
    send_ref[...] = grad.astype(BF16)


def make_attend_back(length, width, rows, chunks):
    scale = 1.0 / math.sqrt(HD)

    def body(places, spots, cos_ref, sin_ref, *refs):
        blocks, refs = refs[:4], refs[4:]
        normed, weight, qkv, att, lse = refs[:5]
        d_pre = refs[5]
        outs = refs[6:-11]
        resid, grad, k_pad, k2_pad, v_pad, v2_pad, da, dk, dk2, dv, dv2 = refs[-11:]
        for j in range(4):
            resid[at_block(places, j, rows), :] = blocks[j][...]
        back = dot_nn(resid[...], weight[:, 4 * LANES :])
        lanes = lane_iota((length, LANES))
        is_low = lanes < HD
        da[:, LANES:] = back[:, LANES:].astype(BF16)
        da[:, :LANES] = shift(jnp.where(is_low, 0.0, back[:, :LANES]), HD).astype(BF16)
        fill_padded(k_pad, qkv[:, LANES : 2 * LANES], length)
        fill_padded(
            k2_pad, shift(qkv[:, 2 * LANES : 3 * LANES].astype(F32), HD).astype(BF16), length
        )
        fill_padded(v_pad, qkv[:, 3 * LANES : 4 * LANES], length)
        fill_padded(v2_pad, qkv[:, 4 * LANES : 5 * LANES], length)
        for piece in (dk, dk2, dv, dv2):
            piece[...] = jnp.zeros_like(piece)
        low, high = low_high()
        tile_low = lane_iota((TILE, LANES)) < HD
        cosine, sine = cos_ref[...], sin_ref[...]
        for t in range(length // TILE):
            span = slice(t * TILE, (t + 1) * TILE)
            window = slice(t * TILE, (t + 1) * TILE + WINDOW)
            mask = tile_mask(t * TILE, length)
            q_main, q_rest = qkv[span, 0:LANES], qkv[span, 2 * LANES : 3 * LANES]
            da_main, da_rest = da[span, LANES:], da[span, :LANES]
            main = da_main.astype(F32) * att[span, LANES:].astype(F32)
            rest = da_rest.astype(F32) * shift(att[span, :LANES].astype(F32), HD)
            deltas = (
                jnp.sum(jnp.where(tile_low, main, 0.0), axis=-1, keepdims=True),
                jnp.sum(jnp.where(tile_low, 0.0, main), axis=-1, keepdims=True),
                jnp.sum(jnp.where(tile_low, rest, 0.0), axis=-1, keepdims=True),
            )
            d_query = []
            for h, (q, d, k_ref, v_ref, dk_ref, dv_ref) in enumerate(
                (
                    (q_main * low, da_main * low, k_pad, v_pad, dk, dv),
                    (q_main * high, da_main * high, k_pad, v_pad, dk, dv),
                    (q_rest * low, da_rest * low, k2_pad, v2_pad, dk2, dv2),
                )
            ):
                keys = k_ref[window, :]
                score = jnp.where(mask, dot_nt(q, keys) * scale, MASKED)
                probs = jnp.exp(score - lse[span, h : h + 1])
                d_probs = dot_nt(d, v_ref[window, :])
                d_score = (probs * (d_probs - deltas[h]) * scale).astype(BF16)
                d_query.append(dot_nn(d_score, keys))
                dk_ref[window, :] += dot_tn(d_score, q)
                dv_ref[window, :] += dot_tn(probs.astype(BF16), d)
            d_main = jnp.where(tile_low, d_query[0], d_query[1])
            d_pre[span, 0:LANES] = turn(d_main, cosine[span], sine[span], True).astype(BF16)
            grad[span, 0:LANES] = jnp.where(tile_low, d_query[2], 0.0)
        inside = slice(HALF, HALF + length)
        d_pre[:, LANES : 2 * LANES] = turn(dk[inside, :], cosine, sine, True).astype(BF16)
        rest = jnp.where(is_low, grad[0:length, 0:LANES], shift(dk2[inside, :], HD))
        d_pre[:, 2 * LANES : 3 * LANES] = turn(rest, cosine, sine, True).astype(BF16)
        d_pre[:, 3 * LANES : 4 * LANES] = dv[inside, :].astype(BF16)
        d_pre[:, 4 * LANES : 5 * LANES] = dv2[inside, :].astype(BF16)
        triple = dot_tn(normed[...], d_pre[...])
        merge = dot_tn(resid[...], att[...])
        grad[:, : 4 * LANES] = triple[:, : 4 * LANES]
        grad[:, 4 * LANES : 5 * LANES] = triple[:, 4 * LANES :] + merge[:, :LANES]
        grad[:, 5 * LANES :] = merge[:, LANES:]
        spread_chunks(grad, spots, outs, width // chunks, chunks)

    return body


def make_input_share(rows):
    def body(places, d_pre, weight, keep, send, partial):
        partial[...] = dot_nt(d_pre[...], weight[:, : 5 * LANES])
        for i, j in enumerate((0, 2)):
            keep[i] = partial[at_block(places, j, rows), :]
        for i, j in enumerate((1, 3)):
            send[i] = partial[at_block(places, j, rows), :].astype(BF16)

    return body


def finish_kernel(
    rows_ref, d_residual_ref, mine_ref, got_ref, residual_ref, out_mine, out_got, grad_ref, out_ref
):
    normed, scale = row_stats(rows_ref[...])
    scaled = mine_ref[...] + got_ref[...].astype(F32)
    grad_ref[...] = d_residual_ref[...] + scaled_back(scaled, normed, scale)
    out_ref[...] = residual_ref[...] + out_mine[...] + out_got[...].astype(F32)


def adam_step(weight, first, second, grad, rate):
    first_new = BETA_FIRST * first + (1.0 - BETA_FIRST) * grad
    second_new = BETA_SECOND * second + (1.0 - BETA_SECOND) * grad * grad
    first_hat = first_new / (1.0 - BETA_FIRST**STEP_COUNT)
    second_hat = second_new / (1.0 - BETA_SECOND**STEP_COUNT)
    fresh = weight - rate * (first_hat / (jnp.sqrt(second_hat) + ADAM_EPS) + DECAY * weight)
    return (fresh, first_new, second_new)


def column_of(row):
    count = row.shape[1]
    down = lax.broadcasted_iota(jnp.int32, (count, count), 0)
    along = lax.broadcasted_iota(jnp.int32, (count, count), 1)
    return jnp.sum(jnp.where(down == along, row, 0.0), axis=1, keepdims=True)


def row_of(column):
    count = column.shape[0]
    down = lax.broadcasted_iota(jnp.int32, (count, LANES), 0)
    along = lax.broadcasted_iota(jnp.int32, (count, LANES), 1)
    return jnp.sum(jnp.where(down == along, column, 0.0), axis=0, keepdims=True)


def rounded(value):
    return value.astype(BF16).astype(F32)


def pack_attend_kernel(gain_ref, triple_ref, merge_ref, out_ref):
    gain = column_of(rounded(gain_ref[...]))
    q, k, v = (rounded(triple_ref[c]) * gain for c in range(3))
    merge = merge_ref[...].T
    out_ref[...] = jnp.concatenate(
        [
            q[:, :LANES],
            k[:, :LANES],
            q[:, LANES:],
            k[:, LANES:],
            v[:, :LANES],
            v[:, LANES:],
            merge[:, LANES:],
            merge[:, :LANES],
        ],
        axis=1,
    ).astype(BF16)


def pack_feed_kernel(gain_ref, expand_ref, reduce_ref, out_ref):
    gain = column_of(rounded(gain_ref[...]))
    one, two = (rounded(expand_ref[c]) * gain for c in range(2))
    turned = reduce_ref[...].T
    wide = 2 * LANES
    spare = jnp.zeros((turned.shape[0], LANES // 4), F32)
    out_ref[...] = jnp.concatenate(
        [
            one[:, :wide],
            two[:, :wide],
            one[:, wide:],
            two[:, wide:],
            turned[:, wide:],
            spare,
            turned[:, :wide],
        ],
        axis=1,
    ).astype(BF16)


def total_of(parts):
    total = parts[0][...]
    for part in parts[1:]:
        total = total + part[...].astype(F32)
    return total


def adam_store(index, grad, rate, weight, first, second, grad_out, fresh_out, first_out, second_out):
    fresh, first_new, second_new = adam_step(weight[index], first[index], second[index], grad, rate)
    grad_out[index] = grad
    fresh_out[index] = fresh
    first_out[index] = first_new
    second_out[index] = second_new


def share_of(plain, weight):
    total = jnp.zeros((plain[0].shape[0], 1), F32)
    for c, grad in enumerate(plain):
        total = total + jnp.sum(grad * rounded(weight[c]), axis=1, keepdims=True)
    return row_of(total)


def attend_plain(pack):
    q = jnp.concatenate([pack[:, :LANES], pack[:, 2 * LANES : 2 * LANES + HD]], axis=1)
    k = jnp.concatenate([pack[:, LANES : 2 * LANES], pack[:, 2 * LANES + HD : 3 * LANES]], axis=1)
    v = jnp.concatenate([pack[:, 3 * LANES : 4 * LANES], pack[:, 4 * LANES : 4 * LANES + HD]], axis=1)
    return q, k, v


def make_share(count):
    def body(*refs):
        parts, (weight, other, out) = refs[:count], refs[count:]
        plain = attend_plain(total_of(parts))
        row = lax.broadcasted_iota(jnp.int32, (8, LANES), 0)
        out[...] = jnp.where(row == 0, share_of(plain, weight), other[...])

    return body


def make_adam_attend(count):
    def body(*refs):
        parts, refs = refs[:count], refs[count:]
        gain, refs = refs[0], refs[1:]
        triple, merge = refs[0::2], refs[1::2]
        pack = total_of(parts)
        scale = column_of(rounded(gain[...]))
        for c, grad in enumerate(attend_plain(pack)):
            adam_store(c, grad * scale, RATE_MATRIX, *triple)
        grad = jnp.concatenate([pack[:, 5 * LANES :], pack[:, 4 * LANES + HD : 5 * LANES]], axis=1)
        adam_store(Ellipsis, grad.T, RATE_MATRIX, *merge)

    return body


def make_adam_feed(count):
    def body(*refs):
        parts, refs = refs[:count], refs[count:]
        gain, share, refs = refs[0], refs[-1], refs[1:-1]
        expand, reduce = refs[0::2], refs[1::2]
        pack = total_of(parts)
        wide, part = 2 * LANES, LANES // 4
        rest = pack[:, 4 * LANES : 5 * LANES]
        plain = (
            jnp.concatenate([pack[:, :wide], rest[:, :part]], axis=1),
            jnp.concatenate([pack[:, wide : 2 * wide], rest[:, part : 2 * part]], axis=1),
        )
        share[...] = jnp.broadcast_to(share_of(plain, expand[0]), (8, LANES))
        scale = column_of(rounded(gain[...]))
        for c, grad in enumerate(plain):
            adam_store(c, grad * scale, RATE_MATRIX, *expand)
        grad = jnp.concatenate([pack[:, 5 * LANES :], rest[:, 2 * part : 3 * part]], axis=1)
        adam_store(Ellipsis, grad.T, RATE_MATRIX, *reduce)

    return body


def gain_step_kernel(*refs):
    parts, refs = refs[:4], refs[4:]
    total = parts[0][...] + parts[1][...] + parts[2][...] + parts[3][...]
    count = refs[0].shape[1]
    for i in range(2):
        adam_store(Ellipsis, total[i : i + 1, :count], RATE_GAIN, *refs[i::2])


def pack_attend(gain, triple, merge):
    folded = (gain.astype(BF16).astype(F32)[:, None] * triple.astype(BF16).astype(F32)).astype(BF16)
    turned = merge.astype(BF16).T
    q, k, v = folded[0], folded[1], folded[2]
    return jnp.concatenate(
        [
            q[:, :LANES],
            k[:, :LANES],
            q[:, LANES:],
            k[:, LANES:],
            v[:, :LANES],
            v[:, LANES:],
            turned[:, LANES:],
            turned[:, :LANES],
        ],
        axis=1,
    )


def unpack_attend(pack, gain):
    scale = gain.astype(BF16).astype(F32)[:, None]
    q = jnp.concatenate([pack[:, :LANES], pack[:, 2 * LANES : 2 * LANES + HD]], axis=1)
    k = jnp.concatenate([pack[:, LANES : 2 * LANES], pack[:, 2 * LANES + HD : 3 * LANES]], axis=1)
    v = jnp.concatenate([pack[:, 3 * LANES : 4 * LANES], pack[:, 4 * LANES : 4 * LANES + HD]], axis=1)
    plain = jnp.stack([q, k, v])
    merge = jnp.concatenate([pack[:, 5 * LANES :], pack[:, 4 * LANES + HD : 5 * LANES]], axis=1).T
    return plain, plain * scale, merge


def pack_feed(gain, expand, reduce):
    folded = (gain.astype(BF16).astype(F32)[:, None] * expand.astype(BF16).astype(F32)).astype(BF16)
    turned = reduce.astype(BF16).T
    wide = 2 * LANES
    spare = jnp.zeros((turned.shape[0], LANES // 4), BF16)
    return jnp.concatenate(
        [
            folded[0][:, :wide],
            folded[1][:, :wide],
            folded[0][:, wide:],
            folded[1][:, wide:],
            turned[:, wide:],
            spare,
            turned[:, :wide],
        ],
        axis=1,
    )


def unpack_feed(pack, gain):
    scale = gain.astype(BF16).astype(F32)[:, None]
    wide, part = 2 * LANES, LANES // 4
    rest = pack[:, 4 * LANES : 5 * LANES]
    one = jnp.concatenate([pack[:, :wide], rest[:, :part]], axis=1)
    two = jnp.concatenate([pack[:, wide : 2 * wide], rest[:, part : 2 * part]], axis=1)
    plain = jnp.stack([one, two])
    reduce = jnp.concatenate([pack[:, 5 * LANES :], rest[:, 2 * part : 3 * part]], axis=1).T
    return plain, plain * scale, reduce


def make_on_device(sizes):
    dp, mp = sizes["dp"], sizes["mp"]
    direct = dp == 8

    def over_mp(value, step):
        return lax.ppermute(value, "mp", [(i, i ^ step) for i in range(mp)])

    def over_dp(value, step):
        return lax.ppermute(value, "dp", [(i, i ^ step) for i in range(dp)])

    def gather_chunks(shard):
        if not direct:
            return [lax.all_gather(shard, "dp", axis=0, tiled=True)]
        along = [shard] + [over_dp(shard, s) for s in (2, 4, 6)]
        across = [over_dp(piece, 1) for piece in along]
        return [piece for pair in zip(along, across) for piece in pair]

    def reduce_chunks(chunks):
        if not direct:
            return [lax.psum_scatter(chunks[0], "dp", scatter_dimension=0, tiled=True)]
        groups = len(chunks) // 2
        found = []
        for g in range(groups):
            mine, send = chunks[2 * g], chunks[2 * g + 1]
            got = over_dp(send, 1)
            first = g * mine.shape[0]
            outs = [
                (mine.shape[1:], BF16 if first + i else F32) for i in range(mine.shape[0])
            ]
            sums = run_kernel(chunk_sum_kernel, outs, (mine, got))
            for i, part in enumerate(sums):
                step = 2 * (first + i)
                found.append(over_dp(part, step) if step else part)
        return found

    def reduce_pairs(pairs):
        if not direct:
            return [lax.psum_scatter(pairs[0], "dp", scatter_dimension=0, tiled=True)]
        got = [over_dp(pairs[i], 2 * i) for i in range(1, dp // 2 - 1)]
        mine, send = pairs[-2:]
        shape = mine.shape
        (last,) = run_kernel(near_sum_kernel, [(shape, BF16)], (mine, over_dp(send, 1)))
        last = over_dp(last, dp - 2)
        mine, send = run_kernel(pair_sum_kernel, [(shape, F32), (shape, BF16)], (pairs[0], *got))
        return [mine, over_dp(send, 1), last]

    def on_device(
        block_input,
        out_cotangent,
        gain_attend,
        weight_triple,
        weight_merge,
        gain_feed,
        weight_expand,
        weight_reduce,
        *moments,
    ):
        rows, width = block_input.shape
        length = rows * mp
        chunks = dp if direct else 1
        deep = width // chunks
        me, here = lax.axis_index("mp"), lax.axis_index("dp")
        places = jnp.bitwise_xor(me, jnp.arange(4, dtype=jnp.int32)) * rows
        if direct:
            spots = jnp.bitwise_xor(here, jnp.arange(dp, dtype=jnp.int32)) * deep
        else:
            spots = jnp.zeros((1,), jnp.int32)
        cosine, sine = (jnp.asarray(table) for table in rope_tables(length))

        def spread_rows(value):
            far = over_mp(value, 2)
            near = over_mp(value, 1)
            return [value, near, far, over_mp(far, 1)]

        if direct:
            gain_row, feed_row = gain_attend.reshape(1, deep), gain_feed.reshape(1, deep)
            (first_pack,) = run_kernel(
                pack_attend_kernel,
                [((deep, 6 * LANES), BF16)],
                (gain_row, weight_triple, weight_merge),
            )
            (second_pack,) = run_kernel(
                pack_feed_kernel,
                [((deep, 7 * LANES), BF16)],
                (feed_row, weight_expand, weight_reduce),
            )
        else:
            first_pack = pack_attend(gain_attend, weight_triple, weight_merge)
            second_pack = pack_feed(gain_feed, weight_expand, weight_reduce)
        (own,) = run_kernel(
            prepare_kernel,
            [((rows, 2 * width), BF16)],
            (places, spots, block_input, out_cotangent),
            scalars=2,
        )
        first_chunks = gather_chunks(first_pack)
        blocks = spread_rows(own)
        second_chunks = gather_chunks(second_pack)

        half_rows = (2, rows, width)
        pad = length + WINDOW
        normed, cot, weight, qkv, att, lse, keep, send = run_kernel(
            make_attend(length, width, rows, chunks),
            [
                ((length, width), BF16),
                ((length, width), BF16),
                ((width, 6 * LANES), BF16),
                ((length, 5 * LANES), BF16),
                ((length, 2 * LANES), BF16),
                ((length, LANES), F32),
                (half_rows, F32),
                (half_rows, BF16),
            ],
            (places, spots, cosine, sine, *blocks, *first_chunks),
            scalars=2,
            scratch=[pltpu.VMEM((pad, LANES), BF16)] * 4 + [pltpu.VMEM((length, width), F32)],
        )

        def to_owner(keep, send):
            mine, far = run_kernel(
                core_sum_kernel,
                [((rows, width), F32), ((rows, width), BF16)],
                (keep, over_mp(send, 1)),
            )
            return mine, over_mp(far, 2)

        mine, got = to_owner(keep, send)
        residual, normed_two = run_kernel(
            second_norm_kernel,
            [((rows, width), F32), ((rows, width), BF16)],
            (block_input, mine, got),
        )
        blocks = spread_rows(normed_two)
        normed_two_all, d_all, inner_all, keep_s, send_s, keep_o, send_o = run_kernel(
            make_feed(length, width, rows, chunks),
            [
                ((length, width), BF16),
                ((length, 5 * LANES), BF16),
                ((length, 3 * LANES), BF16),
                (half_rows, F32),
                (half_rows, BF16),
                (half_rows, F32),
                (half_rows, BF16),
            ],
            (places, spots, *blocks, cot, *second_chunks),
            scalars=2,
            scratch=[pltpu.VMEM((width, 7 * LANES), BF16), pltpu.VMEM((length, width), F32)],
        )
        mine, got = to_owner(keep_s, send_s)
        out_mine, out_got = to_owner(keep_o, send_o)
        feed_chunks = run_kernel(
            make_feed_grads(chunks),
            pair_outs(chunks, deep, 7 * LANES),
            (spots, normed_two_all, cot, d_all, inner_all),
            scalars=1,
            scratch=[pltpu.VMEM((width, 7 * LANES), F32)],
        )
        d_residual, residual_b = run_kernel(
            residual_back_kernel,
            [((rows, width), F32), ((rows, width), BF16)],
            (out_cotangent, residual, mine, got),
        )
        blocks = spread_rows(residual_b)
        feed_parts = reduce_pairs(feed_chunks)
        d_pre, *attend_chunks = run_kernel(
            make_attend_back(length, width, rows, chunks),
            [((length, 5 * LANES), BF16)] + chunk_outs(chunks, deep, 6 * LANES, 2),
            (places, spots, cosine, sine, *blocks, normed, weight, qkv, att, lse),
            scalars=2,
            scratch=[
                pltpu.VMEM((length, width), BF16),
                pltpu.VMEM((width, 6 * LANES), F32),
            ]
            + [pltpu.VMEM((pad, LANES), BF16)] * 4
            + [pltpu.VMEM((length, 2 * LANES), BF16)]
            + [pltpu.VMEM((pad, LANES), F32)] * 4,
        )
        attend_parts = reduce_chunks(attend_chunks)
        keep, send = run_kernel(
            make_input_share(rows),
            [(half_rows, F32), (half_rows, BF16)],
            (places, d_pre, weight),
            scalars=1,
            scratch=[pltpu.VMEM((length, width), F32)],
        )
        mine, got = to_owner(keep, send)
        input_grad, block_output = run_kernel(
            finish_kernel,
            [((rows, width), F32), ((rows, width), F32)],
            (block_input, d_residual, mine, got, residual, out_mine, out_got),
            final=True,
        )

        if direct:
            shapes = [item.shape for item in (weight_expand, weight_reduce)]
            *feed_new, share = run_kernel(
                make_adam_feed(len(feed_parts)),
                [(shape, F32) for shape in shapes * 4] + [((8, LANES), F32)],
                (*feed_parts, feed_row, weight_expand, weight_reduce)
                + (moments[4], moments[5], moments[10], moments[11]),
                final=True,
            )

            (share,) = run_kernel(
                make_share(len(attend_parts)),
                [((8, LANES), F32)],
                (*attend_parts, weight_triple, share),
            )
            got = [over_mp(share, step) for step in (2, 3, 1)]
            gain_new = run_kernel(
                gain_step_kernel,
                [((1, deep), F32)] * 8,
                (share, *got, gain_row, feed_row)
                + tuple(moments[i].reshape(1, deep) for i in (0, 3, 6, 9)),
                final=True,
            )
            shapes = [item.shape for item in (weight_triple, weight_merge)]
            attend_new = run_kernel(
                make_adam_attend(len(attend_parts)),
                [(shape, F32) for shape in shapes * 4],
                (*attend_parts, gain_row, weight_triple, weight_merge)
                + (moments[1], moments[2], moments[7], moments[8]),
                final=True,
            )
            gain_new = [item.reshape(deep) for item in gain_new]
            grads, fresh, first_new, second_new = (
                (gain_new[i], attend_new[i], attend_new[i + 1])
                + (gain_new[i + 1], feed_new[i], feed_new[i + 1])
                for i in (0, 2, 4, 6)
            )
        else:
            plain_triple, grad_triple, grad_merge = unpack_attend(attend_parts[0], gain_attend)
            plain_expand, grad_expand, grad_reduce = unpack_feed(feed_parts[0], gain_feed)
            grads = (
                lax.psum(jnp.sum(plain_triple * rounded(weight_triple), axis=(0, 2)), "mp"),
                grad_triple,
                grad_merge,
                lax.psum(jnp.sum(plain_expand * rounded(weight_expand), axis=(0, 2)), "mp"),
                grad_expand,
                grad_reduce,
            )
            weights = (gain_attend, weight_triple, weight_merge)
            weights += (gain_feed, weight_expand, weight_reduce)
            rates = (RATE_GAIN, RATE_MATRIX, RATE_MATRIX) * 2
            stepped = [
                adam_step(weight, first, second, grad, rate)
                for weight, first, second, grad, rate in zip(
                    weights, moments[:6], moments[6:], grads, rates
                )
            ]
            fresh, first_new, second_new = (tuple(item[i] for item in stepped) for i in range(3))
        return (block_output, input_grad) + grads + fresh + first_new + second_new

    return on_device


def solution(mesh):
    rows = P(("dp", "mp"), None)
    params = (P("dp"), P(None, "dp", "mp"), P("mp", "dp"), P("dp"), P(None, "dp", "mp"), P("mp", "dp"))
    sizes = dict(mesh.shape)
    inner = make_on_device(sizes)

    return jax.shard_map(
        inner,
        mesh=mesh,
        in_specs=(rows, rows) + params * 3,
        out_specs=(rows, rows) + params * 4,
        check_vma=False,
    )
```

```python
import math

import jax
import jax.numpy as jnp
import numpy as np
from jax import lax
from jax.experimental import pallas as pl
from jax.experimental.pallas import tpu as pltpu
from jax.sharding import PartitionSpec as P


HD = 64
WINDOW = 128
HALF = WINDOW // 2
TILE = 128
LANES = 128

NORM_EPS = 1e-05
ROPE_BASE = 10000.0
BETA_FIRST = 0.9
BETA_SECOND = 0.999
ADAM_EPS = 1e-08
DECAY = 0.01
RATE_MATRIX = 0.02
RATE_GAIN = 0.2
STEP_COUNT = 3.0
MASKED = -1e30

INTERPRET = False
F32 = jnp.float32
BF16 = jnp.bfloat16


def run_kernel(body, outs, args, scalars=0, scratch=(), limit=24, final=False, space=pltpu.VMEM):
    in_specs = [pl.BlockSpec(memory_space=pltpu.SMEM)] * scalars
    in_specs += [pl.BlockSpec(memory_space=space)] * (len(args) - scalars)
    out_shape = [jax.ShapeDtypeStruct(shape, kind) for shape, kind in outs]
    if not INTERPRET:
        args = args[:scalars] + tuple(
            pltpu.with_memory_space_constraint(item, space) for item in args[scalars:]
        )
        if not final:
            out_shape = [pltpu.VMEM(shape, kind) for shape, kind in outs]
    return pl.pallas_call(
        body,
        out_shape=out_shape,
        in_specs=in_specs,
        out_specs=[pl.BlockSpec(memory_space=pltpu.VMEM)] * len(outs),
        scratch_shapes=list(scratch),
        interpret=INTERPRET,
        compiler_params=pltpu.CompilerParams(vmem_limit_bytes=limit << 20),
    )(*args)


def dot_nn(left, right):
    return lax.dot_general(left, right, (((1,), (0,)), ((), ())), preferred_element_type=F32)


def dot_nt(left, right):
    return lax.dot_general(left, right, (((1,), (1,)), ((), ())), preferred_element_type=F32)


def dot_tn(left, right):
    return lax.dot_general(left, right, (((0,), (0,)), ((), ())), preferred_element_type=F32)


def lane_iota(shape):
    return lax.broadcasted_iota(jnp.int32, shape, len(shape) - 1)


def shift(value, amount):
    return pltpu.roll(value, amount, 1)


def rope_tables(length):
    half = HD // 2
    freqs = np.power(np.float64(ROPE_BASE), -2.0 * np.arange(half) / HD)
    angles = np.arange(length)[:, None] * freqs[None, :]
    tile = LANES // half
    return (
        np.tile(np.cos(angles), (1, tile)).astype(np.float32),
        np.tile(np.sin(angles), (1, tile)).astype(np.float32),
    )


def turn(value, cosine, sine, back):
    lanes = lane_iota(value.shape)
    first = (lanes % HD) < HD // 2
    ahead = shift(value, LANES - HD // 2)
    behind = shift(value, HD // 2)
    if back:
        other = jnp.where(first, ahead, -behind)
    else:
        other = jnp.where(first, -ahead, behind)
    return value * cosine + other * sine


def gelu_parts(value):
    normal_share = 0.5 * (1.0 + lax.erf(value * (1.0 / math.sqrt(2.0))))
    density = jnp.exp(-0.5 * value * value) * (1.0 / math.sqrt(2.0 * math.pi))
    return (value * normal_share, normal_share + value * density)


def row_stats(rows):
    center = rows - jnp.mean(rows, axis=-1, keepdims=True)
    scale = lax.rsqrt(jnp.mean(center * center, axis=-1, keepdims=True) + NORM_EPS)
    return center * scale, scale


def scaled_back(scaled, normed, scale):
    return scale * (
        scaled
        - jnp.mean(scaled, axis=-1, keepdims=True)
        - normed * jnp.mean(scaled * normed, axis=-1, keepdims=True)
    )


def at_block(offsets, index, size):
    return pl.ds(pl.multiple_of(offsets[index], size), size)


def tile_mask(start, length):
    row = lax.broadcasted_iota(jnp.int32, (TILE, TILE + WINDOW), 0)
    col = lax.broadcasted_iota(jnp.int32, (TILE, TILE + WINDOW), 1)
    ahead = col - row
    key = col + (start - HALF)
    return (ahead >= 0) & (ahead <= WINDOW) & (key >= 0) & (key < length)


def low_high():
    lanes = lane_iota((1, LANES))
    low = (lanes < HD).astype(F32)
    return low.astype(BF16), (1.0 - low).astype(BF16)


def fill_padded(target, value, length):
    target[0:HALF, :] = jnp.zeros((HALF, LANES), target.dtype)
    target[HALF + length : length + WINDOW, :] = jnp.zeros((HALF, LANES), target.dtype)
    target[HALF : HALF + length, :] = value


def prepare_kernel(places, spots, rows_ref, cot_ref, out_ref):
    width = rows_ref.shape[1]
    normed, _ = row_stats(rows_ref[...])
    out_ref[:, :width] = normed.astype(BF16)
    out_ref[:, width:] = cot_ref[...].astype(BF16)


def make_attend(length, width, rows, chunks):
    scale = 1.0 / math.sqrt(HD)

    def body(places, spots, cos_ref, sin_ref, *refs):
        blocks, refs = refs[:4], refs[4:]
        parts, refs = refs[:chunks], refs[chunks:]
        normed, cot, weight, qkv, att, lse, keep, send = refs[:8]
        k_pad, k2_pad, v_pad, v2_pad, partial = refs[8:]
        deep = width // chunks
        for j in range(4):
            normed[at_block(places, j, rows), :] = blocks[j][:, :width]
            cot[at_block(places, j, rows), :] = blocks[j][:, width:]
        for s in range(chunks):
            weight[at_block(spots, s, deep), :] = parts[s][...]
        pre = dot_nn(normed[...], weight[:, : 5 * LANES])
        cosine, sine = cos_ref[...], sin_ref[...]
        lanes = lane_iota((length, LANES))
        is_low = lanes < HD
        for t in range(3):
            turned = turn(pre[:, t * LANES : (t + 1) * LANES], cosine, sine, False)
            qkv[:, t * LANES : (t + 1) * LANES] = turned.astype(BF16)
            if t == 1:
                fill_padded(k_pad, turned.astype(BF16), length)
            if t == 2:
                fill_padded(k2_pad, shift(turned, HD).astype(BF16), length)
        v_main = pre[:, 3 * LANES : 4 * LANES].astype(BF16)
        v_rest = jnp.where(is_low, pre[:, 4 * LANES : 5 * LANES], 0.0).astype(BF16)
        qkv[:, 3 * LANES : 4 * LANES] = v_main
        qkv[:, 4 * LANES : 5 * LANES] = v_rest
        fill_padded(v_pad, v_main, length)
        fill_padded(v2_pad, v_rest, length)
        low, high = low_high()
        tile_lanes = lane_iota((TILE, LANES))
        tile_low = tile_lanes < HD
        for t in range(length // TILE):
            span = slice(t * TILE, (t + 1) * TILE)
            window = slice(t * TILE, (t + 1) * TILE + WINDOW)
            mask = tile_mask(t * TILE, length)
            q_main, q_rest = qkv[span, 0:LANES], qkv[span, 2 * LANES : 3 * LANES]
            found, totals = [], []
            for q, k_ref, v_ref in (
                (q_main * low, k_pad, v_pad),
                (q_main * high, k_pad, v_pad),
                (q_rest * low, k2_pad, v2_pad),
            ):
                score = jnp.where(mask, dot_nt(q, k_ref[window, :]) * scale, MASKED)
                top = jnp.max(score, axis=-1, keepdims=True)
                total = top + jnp.log(jnp.sum(jnp.exp(score - top), axis=-1, keepdims=True))
                probs = jnp.exp(score - total).astype(BF16)
                found.append(dot_nn(probs, v_ref[window, :]))
                totals.append(total)
            main = jnp.where(tile_low, found[0], found[1])
            rest = shift(jnp.where(tile_low, found[2], 0.0), HD)
            att[span, 0:LANES] = rest.astype(BF16)
            att[span, LANES : 2 * LANES] = main.astype(BF16)
            lse[span, :] = jnp.where(
                tile_lanes == 0, totals[0], jnp.where(tile_lanes == 1, totals[1], totals[2])
            )
        partial[...] = dot_nt(att[...], weight[:, 4 * LANES :])
        for i, j in enumerate((0, 2)):
            keep[i] = partial[at_block(places, j, rows), :]
        for i, j in enumerate((1, 3)):
            send[i] = partial[at_block(places, j, rows), :].astype(BF16)

    return body


def core_sum_kernel(keep_ref, got_ref, mine_ref, send_ref):
    mine_ref[...] = keep_ref[0] + got_ref[0].astype(F32)
    send_ref[...] = (keep_ref[1] + got_ref[1].astype(F32)).astype(BF16)


def second_norm_kernel(rows_ref, mine_ref, got_ref, residual_ref, normed_ref):
    residual = rows_ref[...] + mine_ref[...] + got_ref[...].astype(F32)
    residual_ref[...] = residual
    normed, _ = row_stats(residual)
    normed_ref[...] = normed.astype(BF16)


def make_feed(length, width, rows, chunks):
    def body(places, spots, *refs):
        blocks, refs = refs[:4], refs[4:]
        cot, refs = refs[0], refs[1:]
        parts, refs = refs[:chunks], refs[chunks:]
        normed, d_all, inner_all, keep_s, send_s, keep_o, send_o = refs[:7]
        weight, partial = refs[7:]
        deep = width // chunks
        for j in range(4):
            normed[at_block(places, j, rows), :] = blocks[j][...]
        for s in range(chunks):
            weight[at_block(spots, s, deep), :] = parts[s][...]
        both = dot_nn(normed[...], weight[:, : 5 * LANES])
        d_inner = dot_nn(cot[...], weight[:, 4 * LANES :])
        lanes = lane_iota((length, LANES))
        valid = lanes < LANES // 4
        for t in range(3):
            if t < 2:
                gate = both[:, t * LANES : (t + 1) * LANES]
                up = both[:, (2 + t) * LANES : (3 + t) * LANES]
                slope_in = d_inner[:, (1 + t) * LANES : (2 + t) * LANES]
            else:
                gate = both[:, 4 * LANES : 5 * LANES]
                up = shift(gate, LANES - LANES // 4)
                slope_in = shift(d_inner[:, 0:LANES], LANES // 2)
            value, slope = gelu_parts(gate)
            inner = value * up
            d_gate = slope_in * up * slope
            d_up = slope_in * value
            if t < 2:
                inner_all[:, (1 + t) * LANES : (2 + t) * LANES] = inner.astype(BF16)
                d_all[:, t * LANES : (t + 1) * LANES] = d_gate.astype(BF16)
                d_all[:, (2 + t) * LANES : (3 + t) * LANES] = d_up.astype(BF16)
            else:
                inner_all[:, 0:LANES] = shift(
                    jnp.where(valid, inner, 0.0), LANES // 2
                ).astype(BF16)
                d_all[:, 4 * LANES : 5 * LANES] = jnp.where(
                    valid, d_gate, shift(jnp.where(valid, d_up, 0.0), LANES // 4)
                ).astype(BF16)
        partial[...] = dot_nt(d_all[...], weight[:, : 5 * LANES])
        for i, j in enumerate((0, 2)):
            keep_s[i] = partial[at_block(places, j, rows), :]
        for i, j in enumerate((1, 3)):
            send_s[i] = partial[at_block(places, j, rows), :].astype(BF16)
        partial[...] = dot_nt(inner_all[...], weight[:, 4 * LANES :])
        for i, j in enumerate((0, 2)):
            keep_o[i] = partial[at_block(places, j, rows), :]
        for i, j in enumerate((1, 3)):
            send_o[i] = partial[at_block(places, j, rows), :].astype(BF16)

    return body


def group_steps(chunks):
    count = chunks // 2
    return [tuple(range(count - 2))] + [(count - 2,), (count - 1,)]


def spread_chunks(grad, spots, outs, deep, chunks):
    if chunks == 1:
        outs[0][...] = grad[...]
        return
    for g, steps in enumerate(group_steps(chunks)):
        mine, send = outs[2 * g], outs[2 * g + 1]
        for place, i in enumerate(steps):
            mine[place] = grad[at_block(spots, 2 * i, deep), :]
            send[place] = grad[at_block(spots, 2 * i + 1, deep), :].astype(BF16)


def chunk_outs(chunks, deep, lanes):
    if chunks == 1:
        return [((deep, lanes), F32)]
    outs = []
    for steps in group_steps(chunks):
        shape = (len(steps), deep, lanes)
        outs += [(shape, F32), (shape, BF16)]
    return outs


def chunk_sum_kernel(mine_ref, got_ref, *outs):
    for i, out in enumerate(outs):
        out[...] = (mine_ref[i] + got_ref[i].astype(F32)).astype(out.dtype)


def spread_pairs(grad, spots, outs, deep, chunks):
    if chunks == 1:
        outs[0][...] = grad[...]
        return
    steps = [i for i in range(chunks // 2) if i != chunks // 2 - 2]
    for i, out in zip(steps, outs):
        for side in range(2):
            out[side] = grad[at_block(spots, 2 * i + side, deep), :].astype(out.dtype)
    outs[-2][...] = grad[at_block(spots, chunks - 4, deep), :]
    outs[-1][...] = grad[at_block(spots, chunks - 3, deep), :].astype(BF16)


def pair_outs(chunks, deep, lanes):
    if chunks == 1:
        return [((deep, lanes), F32)]
    pairs = [((2, deep, lanes), BF16 if i else F32) for i in range(chunks // 2 - 1)]
    return pairs + [((deep, lanes), F32), ((deep, lanes), BF16)]


def near_sum_kernel(mine, got, out):
    out[...] = (mine[...] + got[...].astype(F32)).astype(out.dtype)


def pair_sum_kernel(*refs):
    parts, (mine, send) = refs[:-2], refs[-2:]
    for side, out in enumerate((mine, send)):
        total = parts[0][side]
        for part in parts[1:]:
            total = total + part[side].astype(F32)
        out[...] = total.astype(out.dtype)


def make_feed_grads(chunks):
    def body(spots, normed, cot, d_all, inner_all, *refs):
        outs, grad = refs[:-1], refs[-1]
        expand = dot_tn(normed[...], d_all[...])
        reduce = dot_tn(cot[...], inner_all[...])
        grad[:, : 4 * LANES] = expand[:, : 4 * LANES]
        grad[:, 4 * LANES : 5 * LANES] = expand[:, 4 * LANES :] + reduce[:, :LANES]
        grad[:, 5 * LANES :] = reduce[:, LANES:]
        spread_pairs(grad, spots, outs, grad.shape[0] // chunks, chunks)

    return body


def residual_back_kernel(cot_ref, residual_ref, mine_ref, got_ref, grad_ref, send_ref):
    normed, scale = row_stats(residual_ref[...])
    scaled = mine_ref[...] + got_ref[...].astype(F32)
    grad = cot_ref[...] + scaled_back(scaled, normed, scale)
    grad_ref[...] = grad
    send_ref[...] = grad.astype(BF16)


def make_attend_back(length, width, rows, chunks):
    scale = 1.0 / math.sqrt(HD)

    def body(places, spots, cos_ref, sin_ref, *refs):
        blocks, refs = refs[:4], refs[4:]
        normed, weight, qkv, att, lse = refs[:5]
        d_pre = refs[5]
        outs = refs[6:-11]
        resid, grad, k_pad, k2_pad, v_pad, v2_pad, da, dk, dk2, dv, dv2 = refs[-11:]
        for j in range(4):
            resid[at_block(places, j, rows), :] = blocks[j][...]
        back = dot_nn(resid[...], weight[:, 4 * LANES :])
        lanes = lane_iota((length, LANES))
        is_low = lanes < HD
        da[:, LANES:] = back[:, LANES:].astype(BF16)
        da[:, :LANES] = shift(jnp.where(is_low, 0.0, back[:, :LANES]), HD).astype(BF16)
        fill_padded(k_pad, qkv[:, LANES : 2 * LANES], length)
        fill_padded(
            k2_pad, shift(qkv[:, 2 * LANES : 3 * LANES].astype(F32), HD).astype(BF16), length
        )
        fill_padded(v_pad, qkv[:, 3 * LANES : 4 * LANES], length)
        fill_padded(v2_pad, qkv[:, 4 * LANES : 5 * LANES], length)
        for piece in (dk, dk2, dv, dv2):
            piece[...] = jnp.zeros_like(piece)
        low, high = low_high()
        tile_low = lane_iota((TILE, LANES)) < HD
        cosine, sine = cos_ref[...], sin_ref[...]
        for t in range(length // TILE):
            span = slice(t * TILE, (t + 1) * TILE)
            window = slice(t * TILE, (t + 1) * TILE + WINDOW)
            mask = tile_mask(t * TILE, length)
            q_main, q_rest = qkv[span, 0:LANES], qkv[span, 2 * LANES : 3 * LANES]
            da_main, da_rest = da[span, LANES:], da[span, :LANES]
            main = da_main.astype(F32) * att[span, LANES:].astype(F32)
            rest = da_rest.astype(F32) * shift(att[span, :LANES].astype(F32), HD)
            deltas = (
                jnp.sum(jnp.where(tile_low, main, 0.0), axis=-1, keepdims=True),
                jnp.sum(jnp.where(tile_low, 0.0, main), axis=-1, keepdims=True),
                jnp.sum(jnp.where(tile_low, rest, 0.0), axis=-1, keepdims=True),
            )
            d_query = []
            for h, (q, d, k_ref, v_ref, dk_ref, dv_ref) in enumerate(
                (
                    (q_main * low, da_main * low, k_pad, v_pad, dk, dv),
                    (q_main * high, da_main * high, k_pad, v_pad, dk, dv),
                    (q_rest * low, da_rest * low, k2_pad, v2_pad, dk2, dv2),
                )
            ):
                keys = k_ref[window, :]
                score = jnp.where(mask, dot_nt(q, keys) * scale, MASKED)
                probs = jnp.exp(score - lse[span, h : h + 1])
                d_probs = dot_nt(d, v_ref[window, :])
                d_score = (probs * (d_probs - deltas[h]) * scale).astype(BF16)
                d_query.append(dot_nn(d_score, keys))
                dk_ref[window, :] += dot_tn(d_score, q)
                dv_ref[window, :] += dot_tn(probs.astype(BF16), d)
            d_main = jnp.where(tile_low, d_query[0], d_query[1])
            d_pre[span, 0:LANES] = turn(d_main, cosine[span], sine[span], True).astype(BF16)
            grad[span, 0:LANES] = jnp.where(tile_low, d_query[2], 0.0)
        inside = slice(HALF, HALF + length)
        d_pre[:, LANES : 2 * LANES] = turn(dk[inside, :], cosine, sine, True).astype(BF16)
        rest = jnp.where(is_low, grad[0:length, 0:LANES], shift(dk2[inside, :], HD))
        d_pre[:, 2 * LANES : 3 * LANES] = turn(rest, cosine, sine, True).astype(BF16)
        d_pre[:, 3 * LANES : 4 * LANES] = dv[inside, :].astype(BF16)
        d_pre[:, 4 * LANES : 5 * LANES] = dv2[inside, :].astype(BF16)
        triple = dot_tn(normed[...], d_pre[...])
        merge = dot_tn(resid[...], att[...])
        grad[:, : 4 * LANES] = triple[:, : 4 * LANES]
        grad[:, 4 * LANES : 5 * LANES] = triple[:, 4 * LANES :] + merge[:, :LANES]
        grad[:, 5 * LANES :] = merge[:, LANES:]
        spread_chunks(grad, spots, outs, width // chunks, chunks)

    return body


def make_input_share(rows):
    def body(places, d_pre, weight, keep, send, partial):
        partial[...] = dot_nt(d_pre[...], weight[:, : 5 * LANES])
        for i, j in enumerate((0, 2)):
            keep[i] = partial[at_block(places, j, rows), :]
        for i, j in enumerate((1, 3)):
            send[i] = partial[at_block(places, j, rows), :].astype(BF16)

    return body


def finish_kernel(
    rows_ref, d_residual_ref, mine_ref, got_ref, residual_ref, out_mine, out_got, grad_ref, out_ref
):
    normed, scale = row_stats(rows_ref[...])
    scaled = mine_ref[...] + got_ref[...].astype(F32)
    grad_ref[...] = d_residual_ref[...] + scaled_back(scaled, normed, scale)
    out_ref[...] = residual_ref[...] + out_mine[...] + out_got[...].astype(F32)


def adam_step(weight, first, second, grad, rate):
    first_new = BETA_FIRST * first + (1.0 - BETA_FIRST) * grad
    second_new = BETA_SECOND * second + (1.0 - BETA_SECOND) * grad * grad
    first_hat = first_new / (1.0 - BETA_FIRST**STEP_COUNT)
    second_hat = second_new / (1.0 - BETA_SECOND**STEP_COUNT)
    fresh = weight - rate * (first_hat / (jnp.sqrt(second_hat) + ADAM_EPS) + DECAY * weight)
    return (fresh, first_new, second_new)


def column_of(row):
    count = row.shape[1]
    down = lax.broadcasted_iota(jnp.int32, (count, count), 0)
    along = lax.broadcasted_iota(jnp.int32, (count, count), 1)
    return jnp.sum(jnp.where(down == along, row, 0.0), axis=1, keepdims=True)


def row_of(column):
    count = column.shape[0]
    down = lax.broadcasted_iota(jnp.int32, (count, LANES), 0)
    along = lax.broadcasted_iota(jnp.int32, (count, LANES), 1)
    return jnp.sum(jnp.where(down == along, column, 0.0), axis=0, keepdims=True)


def rounded(value):
    return value.astype(BF16).astype(F32)


def pack_attend_kernel(gain_far, triple_far, merge_far, out_ref, gain_ref, triple_ref, merge_ref, sems):
    pairs = [(gain_far, gain_ref), (merge_far, merge_ref)]
    pairs += [(triple_far.at[c], triple_ref.at[c]) for c in range(3)]
    copies = [
        pltpu.make_async_copy(source, target, sems.at[i])
        for i, (source, target) in enumerate(pairs)
    ]
    for copy in copies:
        copy.start()
    for copy in copies:
        copy.wait()
    gain = column_of(rounded(gain_ref[...]))
    q, k, v = (rounded(triple_ref[c]) * gain for c in range(3))
    merge = merge_ref[...].T
    out_ref[...] = jnp.concatenate(
        [
            q[:, :LANES],
            k[:, :LANES],
            q[:, LANES:],
            k[:, LANES:],
            v[:, :LANES],
            v[:, LANES:],
            merge[:, LANES:],
            merge[:, :LANES],
        ],
        axis=1,
    ).astype(BF16)


def pack_feed_kernel(gain_ref, expand_ref, reduce_ref, out_ref):
    gain = column_of(rounded(gain_ref[...]))
    one, two = (rounded(expand_ref[c]) * gain for c in range(2))
    turned = reduce_ref[...].T
    wide = 2 * LANES
    spare = jnp.zeros((turned.shape[0], LANES // 4), F32)
    out_ref[...] = jnp.concatenate(
        [
            one[:, :wide],
            two[:, :wide],
            one[:, wide:],
            two[:, wide:],
            turned[:, wide:],
            spare,
            turned[:, :wide],
        ],
        axis=1,
    ).astype(BF16)


def total_of(parts):
    total = parts[0][...]
    for part in parts[1:]:
        total = total + part[...].astype(F32)
    return total


def adam_store(index, grad, rate, weight, first, second, grad_out, fresh_out, first_out, second_out):
    fresh, first_new, second_new = adam_step(weight[index], first[index], second[index], grad, rate)
    grad_out[index] = grad
    fresh_out[index] = fresh
    first_out[index] = first_new
    second_out[index] = second_new


def share_of(plain, weight):
    total = jnp.zeros((plain[0].shape[0], 1), F32)
    for c, grad in enumerate(plain):
        total = total + jnp.sum(grad * rounded(weight[c]), axis=1, keepdims=True)
    return row_of(total)


def attend_plain(pack):
    q = jnp.concatenate([pack[:, :LANES], pack[:, 2 * LANES : 2 * LANES + HD]], axis=1)
    k = jnp.concatenate([pack[:, LANES : 2 * LANES], pack[:, 2 * LANES + HD : 3 * LANES]], axis=1)
    v = jnp.concatenate([pack[:, 3 * LANES : 4 * LANES], pack[:, 4 * LANES : 4 * LANES + HD]], axis=1)
    return q, k, v


def make_share(count):
    def body(*refs):
        parts, (weight, other, out) = refs[:count], refs[count:]
        plain = attend_plain(total_of(parts))
        row = lax.broadcasted_iota(jnp.int32, (8, LANES), 0)
        out[...] = jnp.where(row == 0, share_of(plain, weight), other[...])

    return body


def make_adam_attend(count):
    def body(*refs):
        parts, refs = refs[:count], refs[count:]
        gain, refs = refs[0], refs[1:]
        triple, merge = refs[0::2], refs[1::2]
        pack = total_of(parts)
        scale = column_of(rounded(gain[...]))
        for c, grad in enumerate(attend_plain(pack)):
            adam_store(c, grad * scale, RATE_MATRIX, *triple)
        grad = jnp.concatenate([pack[:, 5 * LANES :], pack[:, 4 * LANES + HD : 5 * LANES]], axis=1)
        adam_store(Ellipsis, grad.T, RATE_MATRIX, *merge)

    return body


def make_adam_feed(count):
    def body(*refs):
        parts, refs = refs[:count], refs[count:]
        gain, share, refs = refs[0], refs[-1], refs[1:-1]
        expand, reduce = refs[0::2], refs[1::2]
        pack = total_of(parts)
        wide, part = 2 * LANES, LANES // 4
        rest = pack[:, 4 * LANES : 5 * LANES]
        plain = (
            jnp.concatenate([pack[:, :wide], rest[:, :part]], axis=1),
            jnp.concatenate([pack[:, wide : 2 * wide], rest[:, part : 2 * part]], axis=1),
        )
        share[...] = jnp.broadcast_to(share_of(plain, expand[0]), (8, LANES))
        scale = column_of(rounded(gain[...]))
        for c, grad in enumerate(plain):
            adam_store(c, grad * scale, RATE_MATRIX, *expand)
        grad = jnp.concatenate([pack[:, 5 * LANES :], rest[:, 2 * part : 3 * part]], axis=1)
        adam_store(Ellipsis, grad.T, RATE_MATRIX, *reduce)

    return body


def gain_step_kernel(*refs):
    parts, refs = refs[:4], refs[4:]
    total = parts[0][...] + parts[1][...] + parts[2][...] + parts[3][...]
    count = refs[0].shape[1]
    for i in range(2):
        adam_store(Ellipsis, total[i : i + 1, :count], RATE_GAIN, *refs[i::2])


def pack_attend(gain, triple, merge):
    folded = (gain.astype(BF16).astype(F32)[:, None] * triple.astype(BF16).astype(F32)).astype(BF16)
    turned = merge.astype(BF16).T
    q, k, v = folded[0], folded[1], folded[2]
    return jnp.concatenate(
        [
            q[:, :LANES],
            k[:, :LANES],
            q[:, LANES:],
            k[:, LANES:],
            v[:, :LANES],
            v[:, LANES:],
            turned[:, LANES:],
            turned[:, :LANES],
        ],
        axis=1,
    )


def unpack_attend(pack, gain):
    scale = gain.astype(BF16).astype(F32)[:, None]
    q = jnp.concatenate([pack[:, :LANES], pack[:, 2 * LANES : 2 * LANES + HD]], axis=1)
    k = jnp.concatenate([pack[:, LANES : 2 * LANES], pack[:, 2 * LANES + HD : 3 * LANES]], axis=1)
    v = jnp.concatenate([pack[:, 3 * LANES : 4 * LANES], pack[:, 4 * LANES : 4 * LANES + HD]], axis=1)
    plain = jnp.stack([q, k, v])
    merge = jnp.concatenate([pack[:, 5 * LANES :], pack[:, 4 * LANES + HD : 5 * LANES]], axis=1).T
    return plain, plain * scale, merge


def pack_feed(gain, expand, reduce):
    folded = (gain.astype(BF16).astype(F32)[:, None] * expand.astype(BF16).astype(F32)).astype(BF16)
    turned = reduce.astype(BF16).T
    wide = 2 * LANES
    spare = jnp.zeros((turned.shape[0], LANES // 4), BF16)
    return jnp.concatenate(
        [
            folded[0][:, :wide],
            folded[1][:, :wide],
            folded[0][:, wide:],
            folded[1][:, wide:],
            turned[:, wide:],
            spare,
            turned[:, :wide],
        ],
        axis=1,
    )


def unpack_feed(pack, gain):
    scale = gain.astype(BF16).astype(F32)[:, None]
    wide, part = 2 * LANES, LANES // 4
    rest = pack[:, 4 * LANES : 5 * LANES]
    one = jnp.concatenate([pack[:, :wide], rest[:, :part]], axis=1)
    two = jnp.concatenate([pack[:, wide : 2 * wide], rest[:, part : 2 * part]], axis=1)
    plain = jnp.stack([one, two])
    reduce = jnp.concatenate([pack[:, 5 * LANES :], rest[:, 2 * part : 3 * part]], axis=1).T
    return plain, plain * scale, reduce


def make_on_device(sizes):
    dp, mp = sizes["dp"], sizes["mp"]
    direct = dp == 8

    def over_mp(value, step):
        return lax.ppermute(value, "mp", [(i, i ^ step) for i in range(mp)])

    def over_dp(value, step):
        return lax.ppermute(value, "dp", [(i, i ^ step) for i in range(dp)])

    def gather_chunks(shard):
        if not direct:
            return [lax.all_gather(shard, "dp", axis=0, tiled=True)]
        along = [shard] + [over_dp(shard, s) for s in (2, 4, 6)]
        across = [over_dp(piece, 1) for piece in along]
        return [piece for pair in zip(along, across) for piece in pair]

    def reduce_chunks(chunks):
        if not direct:
            return [lax.psum_scatter(chunks[0], "dp", scatter_dimension=0, tiled=True)]
        found = []
        for g, steps in enumerate(group_steps(dp)):
            mine, send = chunks[2 * g], chunks[2 * g + 1]
            got = over_dp(send, 1)
            outs = [(mine.shape[1:], BF16 if i else F32) for i in steps]
            sums = run_kernel(chunk_sum_kernel, outs, (mine, got))
            for i, part in zip(steps, sums):
                found.append(over_dp(part, 2 * i) if i else part)
        return found

    def reduce_pairs(pairs):
        if not direct:
            return [lax.psum_scatter(pairs[0], "dp", scatter_dimension=0, tiled=True)]
        steps = [i for i in range(1, dp // 2) if i != dp // 2 - 2]
        got = [over_dp(pair, 2 * i) for i, pair in zip(steps, pairs[1:])]
        mine, send = pairs[-2:]
        shape = mine.shape
        (last,) = run_kernel(near_sum_kernel, [(shape, BF16)], (mine, over_dp(send, 1)))
        last = over_dp(last, dp - 4)
        mine, send = run_kernel(pair_sum_kernel, [(shape, F32), (shape, BF16)], (pairs[0], *got))
        return [mine, over_dp(send, 1), last]

    def on_device(
        block_input,
        out_cotangent,
        gain_attend,
        weight_triple,
        weight_merge,
        gain_feed,
        weight_expand,
        weight_reduce,
        *moments,
    ):
        rows, width = block_input.shape
        length = rows * mp
        chunks = dp if direct else 1
        deep = width // chunks
        me, here = lax.axis_index("mp"), lax.axis_index("dp")
        places = jnp.bitwise_xor(me, jnp.arange(4, dtype=jnp.int32)) * rows
        if direct:
            spots = jnp.bitwise_xor(here, jnp.arange(dp, dtype=jnp.int32)) * deep
        else:
            spots = jnp.zeros((1,), jnp.int32)
        cosine, sine = (jnp.asarray(table) for table in rope_tables(length))

        def spread_rows(value):
            far = over_mp(value, 2)
            near = over_mp(value, 1)
            return [value, near, far, over_mp(far, 1)]

        if direct:
            gain_row, feed_row = gain_attend.reshape(1, deep), gain_feed.reshape(1, deep)
            (first_pack,) = run_kernel(
                pack_attend_kernel,
                [((deep, 6 * LANES), BF16)],
                (gain_row, weight_triple, weight_merge),
                scratch=[
                    pltpu.VMEM(item.shape, F32) for item in (gain_row, weight_triple, weight_merge)
                ]
                + [pltpu.SemaphoreType.DMA((5,))],
                space=pltpu.HBM,
            )
            (second_pack,) = run_kernel(
                pack_feed_kernel,
                [((deep, 7 * LANES), BF16)],
                (feed_row, weight_expand, weight_reduce),
            )
        else:
            first_pack = pack_attend(gain_attend, weight_triple, weight_merge)
            second_pack = pack_feed(gain_feed, weight_expand, weight_reduce)
        (own,) = run_kernel(
            prepare_kernel,
            [((rows, 2 * width), BF16)],
            (places, spots, block_input, out_cotangent),
            scalars=2,
        )
        first_chunks = gather_chunks(first_pack)
        blocks = spread_rows(own)
        second_chunks = gather_chunks(second_pack)

        half_rows = (2, rows, width)
        pad = length + WINDOW
        normed, cot, weight, qkv, att, lse, keep, send = run_kernel(
            make_attend(length, width, rows, chunks),
            [
                ((length, width), BF16),
                ((length, width), BF16),
                ((width, 6 * LANES), BF16),
                ((length, 5 * LANES), BF16),
                ((length, 2 * LANES), BF16),
                ((length, LANES), F32),
                (half_rows, F32),
                (half_rows, BF16),
            ],
            (places, spots, cosine, sine, *blocks, *first_chunks),
            scalars=2,
            scratch=[pltpu.VMEM((pad, LANES), BF16)] * 4 + [pltpu.VMEM((length, width), F32)],
        )

        def to_owner(keep, send):
            mine, far = run_kernel(
                core_sum_kernel,
                [((rows, width), F32), ((rows, width), BF16)],
                (keep, over_mp(send, 1)),
            )
            return mine, over_mp(far, 2)

        mine, got = to_owner(keep, send)
        residual, normed_two = run_kernel(
            second_norm_kernel,
            [((rows, width), F32), ((rows, width), BF16)],
            (block_input, mine, got),
        )
        blocks = spread_rows(normed_two)
        normed_two_all, d_all, inner_all, keep_s, send_s, keep_o, send_o = run_kernel(
            make_feed(length, width, rows, chunks),
            [
                ((length, width), BF16),
                ((length, 5 * LANES), BF16),
                ((length, 3 * LANES), BF16),
                (half_rows, F32),
                (half_rows, BF16),
                (half_rows, F32),
                (half_rows, BF16),
            ],
            (places, spots, *blocks, cot, *second_chunks),
            scalars=2,
            scratch=[pltpu.VMEM((width, 7 * LANES), BF16), pltpu.VMEM((length, width), F32)],
        )
        mine, got = to_owner(keep_s, send_s)
        out_mine, out_got = to_owner(keep_o, send_o)
        feed_chunks = run_kernel(
            make_feed_grads(chunks),
            pair_outs(chunks, deep, 7 * LANES),
            (spots, normed_two_all, cot, d_all, inner_all),
            scalars=1,
            scratch=[pltpu.VMEM((width, 7 * LANES), F32)],
        )
        d_residual, residual_b = run_kernel(
            residual_back_kernel,
            [((rows, width), F32), ((rows, width), BF16)],
            (out_cotangent, residual, mine, got),
        )
        blocks = spread_rows(residual_b)
        feed_parts = reduce_pairs(feed_chunks)
        d_pre, *attend_chunks = run_kernel(
            make_attend_back(length, width, rows, chunks),
            [((length, 5 * LANES), BF16)] + chunk_outs(chunks, deep, 6 * LANES),
            (places, spots, cosine, sine, *blocks, normed, weight, qkv, att, lse),
            scalars=2,
            scratch=[
                pltpu.VMEM((length, width), BF16),
                pltpu.VMEM((width, 6 * LANES), F32),
            ]
            + [pltpu.VMEM((pad, LANES), BF16)] * 4
            + [pltpu.VMEM((length, 2 * LANES), BF16)]
            + [pltpu.VMEM((pad, LANES), F32)] * 4,
        )
        attend_parts = reduce_chunks(attend_chunks)
        keep, send = run_kernel(
            make_input_share(rows),
            [(half_rows, F32), (half_rows, BF16)],
            (places, d_pre, weight),
            scalars=1,
            scratch=[pltpu.VMEM((length, width), F32)],
        )
        mine, got = to_owner(keep, send)
        input_grad, block_output = run_kernel(
            finish_kernel,
            [((rows, width), F32), ((rows, width), F32)],
            (block_input, d_residual, mine, got, residual, out_mine, out_got),
            final=True,
        )

        if direct:
            shapes = [item.shape for item in (weight_expand, weight_reduce)]
            *feed_new, share = run_kernel(
                make_adam_feed(len(feed_parts)),
                [(shape, F32) for shape in shapes * 4] + [((8, LANES), F32)],
                (*feed_parts, feed_row, weight_expand, weight_reduce)
                + (moments[4], moments[5], moments[10], moments[11]),
                final=True,
            )

            (share,) = run_kernel(
                make_share(len(attend_parts)),
                [((8, LANES), F32)],
                (*attend_parts, weight_triple, share),
            )
            got = [over_mp(share, step) for step in (2, 3, 1)]
            gain_new = run_kernel(
                gain_step_kernel,
                [((1, deep), F32)] * 8,
                (share, *got, gain_row, feed_row)
                + tuple(moments[i].reshape(1, deep) for i in (0, 3, 6, 9)),
                final=True,
            )
            shapes = [item.shape for item in (weight_triple, weight_merge)]
            attend_new = run_kernel(
                make_adam_attend(len(attend_parts)),
                [(shape, F32) for shape in shapes * 4],
                (*attend_parts, gain_row, weight_triple, weight_merge)
                + (moments[1], moments[2], moments[7], moments[8]),
                final=True,
            )
            gain_new = [item.reshape(deep) for item in gain_new]
            grads, fresh, first_new, second_new = (
                (gain_new[i], attend_new[i], attend_new[i + 1])
                + (gain_new[i + 1], feed_new[i], feed_new[i + 1])
                for i in (0, 2, 4, 6)
            )
        else:
            plain_triple, grad_triple, grad_merge = unpack_attend(attend_parts[0], gain_attend)
            plain_expand, grad_expand, grad_reduce = unpack_feed(feed_parts[0], gain_feed)
            grads = (
                lax.psum(jnp.sum(plain_triple * rounded(weight_triple), axis=(0, 2)), "mp"),
                grad_triple,
                grad_merge,
                lax.psum(jnp.sum(plain_expand * rounded(weight_expand), axis=(0, 2)), "mp"),
                grad_expand,
                grad_reduce,
            )
            weights = (gain_attend, weight_triple, weight_merge)
            weights += (gain_feed, weight_expand, weight_reduce)
            rates = (RATE_GAIN, RATE_MATRIX, RATE_MATRIX) * 2
            stepped = [
                adam_step(weight, first, second, grad, rate)
                for weight, first, second, grad, rate in zip(
                    weights, moments[:6], moments[6:], grads, rates
                )
            ]
            fresh, first_new, second_new = (tuple(item[i] for item in stepped) for i in range(3))
        return (block_output, input_grad) + grads + fresh + first_new + second_new

    return on_device


def solution(mesh):
    rows = P(("dp", "mp"), None)
    params = (P("dp"), P(None, "dp", "mp"), P("mp", "dp"), P("dp"), P(None, "dp", "mp"), P("mp", "dp"))
    sizes = dict(mesh.shape)
    inner = make_on_device(sizes)

    return jax.shard_map(
        inner,
        mesh=mesh,
        in_specs=(rows, rows) + params * 3,
        out_specs=(rows, rows) + params * 4,
        check_vma=False,
    )
```
